32 devices in a mesh: dp: 4 (over z), group: 8 (over y, x, core).
Axes of the slice: x: 2, y: 2, z: 4, core: 2. Of those that a mesh axis runs over, the one named last changes fastest.
Arguments:
- qkv: bfloat16 [2048, 1920], P(('dp', 'group')), may hold values from -200 to 200
- embed_grad: bfloat16 [2048, 1280], P(('dp', 'group')), may hold values from -0.59765625 to 0.59765625
- out_weight: bfloat16 [1280, 640], replicated, may hold values from -0.25 to 0.25
- image_len: int32 [4, 8, 8], P('dp'), may hold values from 0 to 8, as said below
- image_order: int32 [4, 8, 8], P('dp', 'group'), may hold values from 0 to 7, each once within a row
- image_cut: int32 [4, 8], P('dp', 'group'), may hold values from 8 to 24
Outputs:
- embeds: bfloat16 [2048, 1280], P(('dp', 'group'))
- qkv_grad: bfloat16 [2048, 1920], P(('dp', 'group'))
- weight_grad: float32 [1280, 640], P('group')
The draws below stay inside these ranges and needn't reach their ends.
Inputs may be any that keep to these rules, and one draw needn't show every extreme that they name: For every replica r and destination d, the sum over sources s of image_len[r, s, d] is exactly 32; 0 means that s sends nothing to d. Each image_order[r, s] names every destination once.
All inputs are finite; a program needn't handle non-finite values.
Results may differ from the reference program's by a relative error of at most 0.017.
Values may be sent and summed in bfloat16 or wider, within the bound.
A program may use at most 64 MiB of HBM per device.

```python
import functools
import math
import jax
import jax.numpy as jnp
from jax import lax

D = 1280
HD = 80
HEADS = 8
SLOT = 8
HF = 640
PACK = 32
SRC_ROWS = 64
ROWS = 2048
N_DP = 4
N_GROUP = 8


def draw_qkv(key, part):
    first = jax.random.fold_in(key, 0)
    base = jnp.clip(jax.random.normal(first, (ROWS, 3 * HF), jnp.float32), -6.0, 6.0)
    return base.astype(jnp.bfloat16)


def draw_image_len(key, part):
    first, second = jax.random.split(key, 2)
    pairs = N_GROUP // 2
    lower = jax.random.randint(first, (N_DP, pairs, 1), 0, SLOT + 1)
    spread = jax.random.randint(second, (N_DP, pairs, N_GROUP), 0, SLOT + 1)
    upper = lower + spread * (SLOT + 1 - lower) // (SLOT + 1)
    pair_index = jnp.arange(pairs, dtype=jnp.int32)[None, :, None]
    dest_index = jnp.arange(N_GROUP, dtype=jnp.int32)[None, None, :]
    upper = jnp.where((pair_index == 0) & (dest_index == 0), SLOT, upper)
    stacked = jnp.stack([upper, SLOT - upper], axis=2)
    return stacked.reshape(N_DP, N_GROUP, N_GROUP).astype(jnp.int32)


def with_ends(array, own_key, smallest, top_value):
    spot = [jax.random.randint(jax.random.fold_in(own_key, axis), (), 0, length) for axis, length in enumerate(array.shape)]
    longest = array.shape.index(max(array.shape))
    neighbour = spot[:longest] + [(spot[longest] + 1) % array.shape[longest]] + spot[longest + 1:]
    return array.at[tuple(spot)].set(smallest).at[tuple(neighbour)].set(top_value)


def raised(drawn, stream_key, source, target, shards_of, factor):
    owner, partner = [(jnp.arange(drawn.shape[dim]) // (drawn.shape[dim] // shards_of)).reshape([-1 if axis == dim else 1 for axis in range(drawn.ndim)]) for dim in (source, target)]
    chosen = jax.random.permutation(stream_key, shards_of)[partner]
    strong = (owner == chosen) | (owner == (partner + shards_of // 2) % shards_of)
    return jnp.where(strong, factor * drawn, drawn)


def steps_of(rng, shape, cuts, smallest, largest):
    loudness, own = 1.0, jax.random.fold_in(rng, 6)
    for dim, blocks in cuts:
        draws = jnp.exp(jax.random.uniform(jax.random.fold_in(own, dim), (blocks,), jnp.float32, smallest / len(cuts), largest / len(cuts)))
        loudness = loudness * jnp.repeat(draws, shape[dim] // blocks).reshape([-1 if axis == dim else 1 for axis in range(len(shape))])
    return loudness


def normal_values(key, extent, deviation, most, pieces=(), kind=jnp.bfloat16):
    values = deviation * jax.random.normal(key, extent, jnp.float32)
    if pieces:
        values = values * steps_of(key, extent, pieces, -0.22, 0.18)
    return jnp.clip(values, -most, most).astype(kind)


def heavy_noise(rng, extent, scale, bound, pieces, heavy, kind=jnp.bfloat16):
    array = scale * jax.random.normal(rng, extent, jnp.float32)
    if pieces:
        array = array * steps_of(rng, extent, pieces, -0.22, 0.18)
    return jnp.clip(raised(array, jax.random.fold_in(rng, 3), *heavy), -bound, bound).astype(kind)


def setup_inputs(seed: int = 0) -> dict:
    seeds = jax.random.split(jax.random.key(seed), 7)
    return {
        "qkv": draw_qkv(jax.random.fold_in(seeds[6], 71), 0),
        "embed_grad": heavy_noise(seeds[1], (ROWS, D), 0.1, 0.59765625, ((0, 32),), (0, 1, 32, 2.75)),
        "out_weight": normal_values(seeds[2], (D, HF), HF ** -0.5, 0.25),
        "image_len": draw_image_len(jax.random.fold_in(seeds[6], 71), 0),
        "image_order": jax.vmap(lambda own: jax.random.permutation(own, N_GROUP))(jax.random.split(seeds[4], N_DP * N_GROUP)).reshape((N_DP, N_GROUP, N_GROUP)).astype(jnp.int32),
        "image_cut": with_ends(jax.random.randint(seeds[5], (N_DP, N_GROUP), N_GROUP * SLOT // 8, 3 * N_GROUP * SLOT // 8 + 1), jax.random.fold_in(seeds[5], 1), N_GROUP * SLOT // 8, (3 * N_GROUP * SLOT // 8 + 1) - 1).astype(jnp.int32),
    }


masked_value = -1e+30

def dest_block(qkv, embed_grad, out_weight, image_len, image_order, image_cut, weight_sum, block):
    replica = (block // N_GROUP).astype(jnp.int32)
    target = (block % N_GROUP).astype(jnp.int32)
    lens = lax.dynamic_index_in_dim(image_len, replica, 0, keepdims=False)
    order = lax.dynamic_index_in_dim(image_order, replica, 0, keepdims=False)
    cut = lax.dynamic_index_in_dim(image_cut.reshape(-1), block, 0, keepdims=False)
    dest_range = jnp.arange(N_GROUP, dtype=jnp.int32)
    onehot = (order[:, :, None] == dest_range[None, None, :]).astype(jnp.int32)
    ordered = lax.optimization_barrier(jnp.sum(onehot * lens[:, None, :], axis=2)).astype(jnp.int32)
    ends = jnp.cumsum(ordered, axis=1).astype(jnp.int32)
    starts = ends - ordered
    dest_start = lax.optimization_barrier(jnp.sum(onehot * starts[:, :, None], axis=1)).astype(jnp.int32)
    column = lax.dynamic_index_in_dim(lens, target, 1, keepdims=False)
    start_col = lax.dynamic_index_in_dim(dest_start, target, 1, keepdims=False)
    col_ends = jnp.cumsum(column).astype(jnp.int32)
    col_starts = col_ends - column
    positions = jnp.arange(PACK, dtype=jnp.int32)
    source_of = lax.optimization_barrier(jnp.sum((col_ends[None, :] <= positions[:, None]).astype(jnp.int32), axis=1)).astype(jnp.int32)
    selector = (source_of[:, None] == dest_range[None, :]).astype(jnp.int32)
    offset = positions - lax.optimization_barrier(jnp.sum(selector * col_starts[None, :], axis=1)).astype(jnp.int32)
    local = lax.optimization_barrier(jnp.sum(selector * start_col[None, :], axis=1)).astype(jnp.int32) + offset
    rows = ((replica * N_GROUP + source_of) * SRC_ROWS + local).astype(jnp.int32)
    qkv_rows = jnp.take(qkv, rows, axis=0)
    cot_rows = jnp.take(embed_grad, rows, axis=0)
    second = positions >= cut
    same = second[:, None] == second[None, :]
    score_scale = 1.0 / math.sqrt(HD)
    query = qkv_rows[:, :HF].astype(jnp.float32).reshape(PACK, HEADS, HD)
    keys = qkv_rows[:, HF:2 * HF].astype(jnp.float32).reshape(PACK, HEADS, HD)
    values = qkv_rows[:, 2 * HF:].astype(jnp.float32).reshape(PACK, HEADS, HD)
    scores = jnp.einsum('qhe,khe->hqk', query, keys) * score_scale
    scores = jnp.where(same[None], scores, masked_value)
    top = lax.optimization_barrier(jnp.max(scores, axis=-1, keepdims=True))
    expo = jnp.exp(scores - top)
    probs = expo / lax.optimization_barrier(jnp.sum(expo, axis=-1, keepdims=True))
    probs_b = probs.astype(jnp.bfloat16)
    attended = jnp.einsum('hqk,khe->qhe', probs_b.astype(jnp.float32), values).astype(jnp.bfloat16)
    attended = attended.reshape(PACK, HF)
    embeds = jnp.dot(attended, out_weight.T, preferred_element_type=jnp.float32).astype(jnp.bfloat16)
    attended_grad = jnp.dot(cot_rows, out_weight, preferred_element_type=jnp.float32).astype(jnp.bfloat16)
    weight_sum = weight_sum + jnp.dot(cot_rows.T, attended, preferred_element_type=jnp.float32)
    grad_heads = attended_grad.astype(jnp.float32).reshape(PACK, HEADS, HD)
    att_heads = attended.astype(jnp.float32).reshape(PACK, HEADS, HD)
    prob_grad = jnp.einsum('qhe,khe->hqk', grad_heads, values)
    delta = jnp.transpose(lax.optimization_barrier(jnp.sum(grad_heads * att_heads, axis=-1)), (1, 0))[:, :, None]
    score_grad = (probs * (prob_grad - delta) * score_scale).astype(jnp.bfloat16).astype(jnp.float32)
    query_grad = jnp.einsum('hqk,khe->qhe', score_grad, keys).astype(jnp.bfloat16)
    keys_grad = jnp.einsum('hqk,qhe->khe', score_grad, query).astype(jnp.bfloat16)
    values_grad = jnp.einsum('hqk,qhe->khe', probs_b.astype(jnp.float32), grad_heads).astype(jnp.bfloat16)
    grads = jnp.concatenate([query_grad.reshape(PACK, HF), keys_grad.reshape(PACK, HF), values_grad.reshape(PACK, HF)], axis=1)
    return (weight_sum, (embeds, grads, rows))

def reference(qkv, embed_grad, out_weight, image_len, image_order, image_cut):
    blocks = jnp.arange(N_DP * N_GROUP, dtype=jnp.int32)
    step_fn = functools.partial(dest_block, qkv, embed_grad, out_weight, image_len, image_order, image_cut)
    weight_sum, outputs = lax.scan(step_fn, jnp.zeros((D, HF), jnp.float32), blocks)
    embeds, grads, rows = outputs
    flat_rows = rows.reshape(-1)
    embeds_all = jnp.zeros((ROWS, D), jnp.bfloat16).at[flat_rows].set(embeds.reshape(-1, D))
    grads_all = jnp.zeros((ROWS, 3 * HF), jnp.bfloat16).at[flat_rows].set(grads.reshape(-1, 3 * HF))
    return (embeds_all, grads_all, weight_sum)
```

```python
import functools
import math

import jax
import jax.numpy as jnp
from jax import lax
from jax.experimental import pallas as pl
from jax.experimental.pallas import tpu as pltpu
from jax.sharding import PartitionSpec as P

HD = 80
HEADS = 8
SLOT = 8
MASKED = -1e30
F32 = jnp.float32
BF16 = jnp.bfloat16
MESH = pl.DeviceIdType.MESH


TRACE = False
G_WHEN = 2
open_scope = []


def mark(name):
    if TRACE:
        if open_scope:
            open_scope.pop().__exit__(None, None, None)
        if name:
            scope = jax.named_scope(name)
            scope.__enter__()
            open_scope.append(scope)


def dot(a, b, dims=((1,), (0,))):
    return lax.dot_general(a, b, (dims, ((), ())), preferred_element_type=F32)


TN = ((0,), (0,))
NT = ((1,), (1,))


def iota(shape, dim):
    return lax.broadcasted_iota(jnp.int32, shape, dim)


def flat(x):
    g, s, c = x.shape
    return x.astype(F32).reshape(g * s, c).astype(BF16)


def partner(me, k):
    out, bit = me, 1
    while bit <= k:
        if k & bit:
            has = lax.rem(lax.div(me, bit), 2)
            out = out + bit * (1 - 2 * has)
        bit *= 2
    return out


def kernel(
    groups, reps,
    len_hbm, order_hbm, cut_hbm, qkv_hbm, cot_hbm, w_hbm,
    emb, grad, own,
    len_ref, order_ref, cut_ref, qkv, cot, w, sel, pack_t,
    sendq, recvq, sendg, recvg, cots, cotr, qbig, gbig, attall,
    grads, backs, backr, cot_t, spread, slot_rows, zsend, zbuf,
    in_sem,
    sq, rq, sg, rg, sc, rc, sa, ra, sb, rb, sz, rz,
):
    me = lax.axis_index("group")
    rep = lax.axis_index("dp")
    rows, feats3 = qkv.shape
    hf = feats3 // 3
    width = cot.shape[1]
    slots = groups * SLOT
    pack = slots // 2
    every = groups * pack
    share = width // groups
    folds = share // cots.shape[1]
    chunks = zbuf.shape[1]

    mark("m00_start")
    barrier = pltpu.get_barrier_semaphore()
    order_k = list(range(groups - 1, 0, -1))
    for k in order_k:
        pl.semaphore_signal(
            barrier, inc=1, device_id={"group": partner(me, k)}, device_id_type=MESH
        )

    blocked = chunks % reps == 0
    if blocked:
        peers = reps - 1
        for d in range(1, reps):
            pl.semaphore_signal(
                barrier, inc=1, device_id={"dp": lax.rem(rep + d, reps)}, device_id_type=MESH
            )
    else:
        peers = (rep > 0).astype(jnp.int32) + (rep < reps - 1).astype(jnp.int32)

        @pl.when(rep > 0)
        def _():
            pl.semaphore_signal(barrier, inc=1, device_id={"dp": rep - 1}, device_id_type=MESH)

        @pl.when(rep < reps - 1)
        def _():
            pl.semaphore_signal(barrier, inc=1, device_id={"dp": rep + 1}, device_id_type=MESH)

    loads = [
        pltpu.make_async_copy(src, dst, in_sem.at[i])
        for i, (src, dst) in enumerate(
            (
                (qkv_hbm, qkv), (cot_hbm, cot), (w_hbm, w),
                (len_hbm, len_ref), (order_hbm, order_ref), (cut_hbm, cut_ref),
            )
        )
    ]
    for i in (3, 4, 0, 1, 2, 5):
        loads[i].start()

    mark("m01_book")
    for i in (3, 4):
        loads[i].wait()
    sub = iota((groups, groups), 0)
    lane = iota((groups, groups), 1)
    eye = sub == lane
    lens = len_ref[...].astype(F32)
    lens_row = jnp.sum(jnp.where(sub == me, lens, 0.0), axis=0, keepdims=True)
    order_row = order_ref[...].astype(F32)
    order_col = jnp.sum(
        jnp.where(eye, jnp.broadcast_to(order_row, eye.shape), 0.0), axis=1, keepdims=True
    )
    onehot = jnp.where(order_col == lane.astype(F32), 1.0, 0.0)
    ordered_col = jnp.sum(onehot * lens_row, axis=1, keepdims=True)
    ordered_row = jnp.sum(jnp.where(eye, ordered_col, 0.0), axis=0, keepdims=True)
    starts_col = jnp.sum(
        jnp.where(lane < sub, jnp.broadcast_to(ordered_row, eye.shape), 0.0),
        axis=1, keepdims=True,
    )
    dest_row = jnp.sum(onehot * starts_col, axis=0, keepdims=True)
    block_of = iota((slots, groups), 0) // SLOT == iota((slots, groups), 1)
    within = lax.rem(iota((slots, 1), 0), SLOT).astype(F32)
    send_start = jnp.sum(jnp.where(block_of, dest_row, 0.0), axis=1, keepdims=True)
    send_len = jnp.sum(jnp.where(block_of, lens_row, 0.0), axis=1, keepdims=True)
    send_pos = jnp.where(within < send_len, send_start + within, -1.0)
    sel[...] = jnp.where(send_pos == iota((slots, rows), 1).astype(F32), 1.0, 0.0).astype(BF16)

    def remote(src, dst, ssem, rsem, k):
        return pltpu.make_async_remote_copy(
            src_ref=src, dst_ref=dst, send_sem=ssem, recv_sem=rsem,
            device_id={"group": partner(me, k)}, device_id_type=MESH,
        )

    def exchange(src, dst, ssem, rsem):
        for k in order_k:
            remote(src.at[partner(me, k)], dst.at[me], ssem, rsem, k).start()
        pltpu.make_async_copy(src.at[me], dst.at[me], rsem).start()

    def arrived(dst, ssem, rsem):
        remote(dst, dst, ssem, rsem, 1).wait_recv()

    def departed(src, ssem, rsem):
        most = src.at[pl.ds(0, groups - 1)]
        remote(most, most, ssem, rsem, 1).wait_send()

    mark("m02_selq")
    loads[0].wait()
    sendq[...] = dot(sel[...], qkv[...]).reshape(groups, SLOT, feats3).astype(BF16)

    mark("m03_barrier")
    pl.semaphore_wait(barrier, groups - 1 + peers)

    mark("m04_sendq")
    exchange(sendq, recvq, sq.at[0], rq.at[0])

    mark("m05_attgrad")
    loads[1].wait()
    loads[2].wait()
    att_grad = dot(cot[...], w[...]).astype(BF16)
    sendg[...] = dot(sel[...], att_grad).reshape(groups, SLOT, hf).astype(BF16)
    mark("m06_cot")
    turned = dot(cot[...], sel[...], ((0,), (1,))).reshape(groups, folds, share // folds, slots)
    cots[...] = jnp.concatenate([turned[:, f] for f in range(folds)], axis=2).astype(BF16)

    mark("m065_book2")
    before = jnp.where(lane < sub, 1.0, 0.0).astype(BF16)
    lens_b = lens.astype(BF16)
    starts = dot(before, lens_b)
    expand = jnp.where(block_of, 1.0, 0.0).astype(BF16)
    starts_me = jnp.sum(jnp.where(lane == me, starts, 0.0), axis=1, keepdims=True).astype(BF16)
    lens_me = jnp.sum(jnp.where(lane == me, lens, 0.0), axis=1, keepdims=True).astype(BF16)
    pos_me = dot(expand, jnp.broadcast_to(starts_me, (groups, pack))) + within
    held_me = within < dot(expand, jnp.broadcast_to(lens_me, (groups, pack)))
    packs = iota((slots, pack), 1).astype(F32)
    pack_t[...] = jnp.where((pos_me == packs) & held_me, 1.0, 0.0).astype(BF16)

    fill = iota((groups, every), 1) // pack == iota((groups, every), 0)
    fill = jnp.where(fill, 1.0, 0.0).astype(BF16)
    first_of = dot(starts.astype(BF16), fill)
    count_of = dot(lens_b, fill)
    place_of = lax.rem(iota((groups, every), 1), pack).astype(F32) - first_of
    place_of = jnp.where((place_of >= 0.0) & (place_of < count_of), place_of, -1.0)
    slot_of = jnp.where(
        place_of >= 0.0, place_of + (iota((groups, every), 1) // pack * SLOT).astype(F32), -1.0
    )
    slot_row = iota((slots, every), 0).astype(F32)
    if folds > 1:
        for s in range(groups):
            spread[s * slots : (s + 1) * slots, :] = jnp.where(
                slot_row == slot_of[s : s + 1, :], 1.0, 0.0
            ).astype(BF16)
    else:
        slot_rows[...] = slot_of
    mine = jnp.sum(
        jnp.where(iota((groups, every), 0) == me, slot_of, 0.0), axis=0, keepdims=True
    )
    home = dot(
        sel[...], jnp.where(slot_row == mine, 1.0, 0.0).astype(BF16), TN
    ).astype(BF16)

    departed(sendq, sq.at[0], rq.at[0])
    exchange(cots, cotr, sc.at[0], rc.at[0])
    if G_WHEN == 0:
        exchange(sendg, recvg, sg.at[0], rg.at[0])

    mark("m07_waitq")
    arrived(recvq, sq.at[0], rq.at[0])
    mark("m08_att")
    loads[5].wait()
    xq = dot(pack_t[...], flat(recvq[...]), TN).astype(BF16)
    query, keys, values = xq[:, :hf], xq[:, hf : 2 * hf], xq[:, 2 * hf :]
    feature = iota((1, hf), 1)
    heads = [
        (feature >= h * HD) & (feature < (h + 1) * HD) for h in range(HEADS)
    ]
    marks = [jnp.where(m, 1.0, 0.0).astype(BF16) for m in heads]
    for h in range(HEADS):
        qbig[h * pack : (h + 1) * pack, :] = query * marks[h]
    scale = 1.0 / math.sqrt(HD)
    cut = cut_ref[...]
    wide = HEADS * pack
    row_second = iota((pack, wide), 0) >= cut
    col_second = lax.rem(iota((pack, wide), 1), pack) >= cut
    same = row_second == col_second
    scores = dot(keys, qbig[...], NT) * scale
    scores = jnp.where(same, scores, MASKED)
    top = jnp.max(scores, axis=0, keepdims=True)
    expo = jnp.exp(scores - top)
    probs = expo / jnp.sum(expo, axis=0, keepdims=True)
    probs_b = probs.astype(BF16)

    def per_head(big):
        out = jnp.where(heads[0], big[:pack], 0.0)
        for h in range(1, HEADS):
            out = jnp.where(heads[h], big[h * pack : (h + 1) * pack], out)
        return out.astype(BF16)

    att = per_head(dot(probs_b, values, TN))
    attall[pl.ds(me, 1)] = att.reshape(1, pack, hf)
    direct = list(range(groups - 2, 0, -2))
    for k in direct:
        remote(attall.at[me], attall.at[me], sa.at[0], ra.at[k // 2], k).start()
    remote(attall.at[me], attall.at[me], sa.at[0], ra.at[0], 1).start()

    if G_WHEN == 1:
        exchange(sendg, recvg, sg.at[0], rg.at[0])

    mark("m11_waitc")
    arrived(cotr, sc.at[0], rc.at[0])
    mark("m12_pack")
    if folds > 1:
        pieces = [cotr[s].astype(F32) for s in range(groups)]
        left = jnp.concatenate(
            [
                jnp.concatenate(
                    [piece[:, f * slots : (f + 1) * slots] for piece in pieces], axis=1
                )
                for f in range(folds)
            ],
            axis=0,
        ).astype(BF16)
        cot_t[...] = dot(left, spread[...]).astype(BF16)
    else:
        cot_t[...] = jnp.zeros(cot_t.shape, BF16)

        def place(s, carry):
            spread[...] = jnp.where(
                slot_row == slot_rows[pl.ds(s, 1), :], 1.0, 0.0
            ).astype(BF16)
            cot_t[...] = cot_t[...] + dot(cotr[s], spread[...]).astype(BF16)
            return carry

        lax.fori_loop(0, groups, place, 0)

    mark("m13_waita")
    for k in direct:
        remote(attall.at[me], attall.at[me], sa.at[0], ra.at[k // 2], k).wait_recv()
        piece = attall.at[partner(me, k)]
        remote(piece, piece, sa.at[0], ra.at[0], 1).start()
    if G_WHEN == 2:
        exchange(sendg, recvg, sg.at[0], rg.at[0])
    half = attall.at[pl.ds(0, groups // 2)]
    remote(half, half, sa.at[0], ra.at[0], 1).wait_recv()
    mark("m14_wg")
    att_rows = attall[...].reshape(every, hf)
    own[...] = dot(cot_t[...], att_rows).reshape(own.shape)

    def backward():
        mark("m09_waitg")
        arrived(recvg, sg.at[0], rg.at[0])
        mark("m10_bwd")
        xg = dot(pack_t[...], flat(recvg[...]), TN).astype(BF16)
        for h in range(HEADS):
            gbig[h * pack : (h + 1) * pack, :] = xg * marks[h]
        prob_grad = dot(values, gbig[...], NT)
        delta = jnp.sum(probs * prob_grad, axis=0, keepdims=True)
        score_grad = (probs * (prob_grad - delta) * scale).astype(BF16)
        grads[:, :hf] = per_head(dot(score_grad, keys, TN))
        grads[:, hf : 2 * hf] = dot(score_grad, qbig[...]).astype(BF16)
        grads[:, 2 * hf :] = dot(probs_b, gbig[...]).astype(BF16)

        backs[...] = dot(pack_t[...], grads[...]).reshape(groups, SLOT, feats3).astype(BF16)
        exchange(backs, backr, sb.at[0], rb.at[0])


    def project():
        mark("m16_emb")
        emb[...] = dot(dot(home, att_rows).astype(BF16), w[...], NT).astype(BF16)

    def source_rows():
        mark("m17_waitb")
        arrived(backr, sb.at[0], rb.at[0])
        mark("m18_back")
        grad[...] = dot(sel[...], flat(backr[...]), TN).astype(BF16)
        mark("m19_z")

    def along_line():
        mark("m15_zchain")
        @pl.when(rep == 0)
        def _():
            zbuf[0] = jnp.zeros(zbuf.shape[1:], BF16)

        @pl.when(rep == reps - 1)
        def _():
            zbuf[1] = jnp.zeros(zbuf.shape[1:], BF16)

        def hop(way, c):
            return pltpu.make_async_remote_copy(
                src_ref=zsend.at[way, c], dst_ref=zbuf.at[way, c],
                send_sem=sz.at[way], recv_sem=rz.at[way, c],
                device_id={"dp": rep + 1 - 2 * way}, device_id_type=MESH,
            )

        def step(way, c):
            spot = rep + way * (reps - 1 - 2 * rep)

            @pl.when(spot > 0)
            def _():
                hop(way, c).wait_recv()

            @pl.when(spot < reps - 1)
            def _():
                zsend[way, c] = (own[c] + zbuf[way, c].astype(F32)).astype(BF16)
                hop(way, c).start()

        near = (rep >= (reps + 1) // 2).astype(jnp.int32)
        edge = (rep == 0) | (rep == reps - 1)

        @pl.when(edge)
        def _():
            for c in range(chunks):
                step(near, c)

        backward()
        project()

        @pl.when(edge)
        def _():
            source_rows()
            for c in range(chunks):
                step(1 - near, c)

        @pl.when(jnp.logical_not(edge))
        def _():
            mark("m19_zmid")
            lag = chunks // 2
            for t in range(chunks + lag):
                if t < chunks:
                    step(near, t)
                if t >= lag:
                    step(1 - near, t - lag)
            source_rows()

        mark("m20_final")
        own[...] = own[...] + zbuf[0].astype(F32) + zbuf[1].astype(F32)

        for way in range(2):
            spot = rep + way * (reps - 1 - 2 * rep)

            @pl.when(spot < reps - 1)
            def _():
                pltpu.make_async_remote_copy(
                    src_ref=zsend.at[way], dst_ref=zbuf.at[way],
                    send_sem=sz.at[way], recv_sem=rz.at[way, 0],
                    device_id={"dp": rep + 1 - 2 * way}, device_id_type=MESH,
                ).wait_send()


    def by_blocks():
        size = chunks // reps
        spread_to = list(range(reps - 1, 0, -2)) + list(range(0, reps, 2))[::-1]

        def across(src, dst, i, to):
            return pltpu.make_async_remote_copy(
                src_ref=src, dst_ref=dst, send_sem=sz.at[i], recv_sem=rz.at[i, 0],
                device_id={"dp": to}, device_id_type=MESH,
            )

        mark("m15_scatter")
        zsend[0] = own[...].astype(BF16)
        for to in spread_to:

            @pl.when(rep != to)
            def _():
                across(
                    zsend.at[0, pl.ds(to * size, size)],
                    zbuf.at[0, pl.ds(rep * size, size)], 0, to,
                ).start()

        block = pl.ds(rep * size, size)
        zbuf[0, block] = jnp.zeros((size,) + zbuf.shape[2:], BF16)
        backward()
        project()
        mark("m17_waits")
        most = zbuf.at[0, pl.ds(0, size * (reps - 1))]
        across(most, most, 0, rep).wait_recv()
        mark("m18_sum")
        total = own[block]
        for r in range(reps):
            total = total + zbuf[0, r * size : (r + 1) * size].astype(F32)
        zbuf[1, block] = total.astype(BF16)
        for to in range(reps):

            @pl.when(rep != to)
            def _():
                across(zbuf.at[1, block], zbuf.at[1, block], 1, to).start()

        source_rows()
        across(most, most, 1, rep).wait_recv()
        mark("m20_final")
        own[...] = zbuf[1].astype(F32)
        for i in range(2):
            across(most, most, i, rep).wait_send()

    if blocked:
        by_blocks()
    else:
        along_line()

    mark("m21_drain")
    departed(sendg, sg.at[0], rg.at[0])
    departed(cots, sc.at[0], rc.at[0])
    departed(backs, sb.at[0], rb.at[0])
    departed(attall, sa.at[0], ra.at[0])
    mark(None)


def write_out(emb, grad, own, emb_hbm, grad_hbm, wg_hbm, sems):
    pairs = ((emb, emb_hbm), (grad, grad_hbm), (own, wg_hbm))
    copies = [
        pltpu.make_async_copy(src, dst, sems.at[i]) for i, (src, dst) in enumerate(pairs)
    ]
    for copy in copies:
        copy.start()
    for copy in copies:
        copy.wait()


def local(groups, reps, qkv, embed_grad, out_weight, image_len, image_order, image_cut):
    rows, feats3 = qkv.shape
    width, hf = out_weight.shape
    slots = groups * SLOT
    pack = slots // 2
    share = width // groups
    part = 8 if share % (8 * reps) == 0 or share % 16 else 16
    chunks = share // part
    folds = 2 if slots < 128 and share % 32 == 0 else 1
    any_space = pl.BlockSpec(memory_space=pl.ANY)
    vmem = pl.BlockSpec(memory_space=pltpu.VMEM)
    dma = pltpu.SemaphoreType.DMA
    emb, grad, wg = pl.pallas_call(
        functools.partial(kernel, groups, reps),
        out_shape=(
            pltpu.VMEM((rows, width), BF16),
            pltpu.VMEM((rows, feats3), BF16),
            pltpu.VMEM((chunks, part, hf), F32),
        ),
        in_specs=[any_space] * 6,
        out_specs=(vmem, vmem, vmem),
        scratch_shapes=[
            pltpu.VMEM((groups, groups), jnp.int32),
            pltpu.VMEM((1, groups), jnp.int32),
            pltpu.VMEM((1, 1), jnp.int32),
            pltpu.VMEM((rows, feats3), BF16),
            pltpu.VMEM((rows, width), BF16),
            pltpu.VMEM((width, hf), BF16),
            pltpu.VMEM((slots, rows), BF16),
            pltpu.VMEM((slots, pack), BF16),
            pltpu.VMEM((groups, SLOT, feats3), BF16),
            pltpu.VMEM((groups, SLOT, feats3), BF16),
            pltpu.VMEM((groups, SLOT, hf), BF16),
            pltpu.VMEM((groups, SLOT, hf), BF16),
            pltpu.VMEM((groups, share // folds, slots * folds), BF16),
            pltpu.VMEM((groups, share // folds, slots * folds), BF16),
            pltpu.VMEM((HEADS * pack, hf), BF16),
            pltpu.VMEM((HEADS * pack, hf), BF16),
            pltpu.VMEM((groups, pack, hf), BF16),
            pltpu.VMEM((pack, feats3), BF16),
            pltpu.VMEM((groups, SLOT, feats3), BF16),
            pltpu.VMEM((groups, SLOT, feats3), BF16),
            pltpu.VMEM((share, groups * pack), BF16),
            pltpu.VMEM((groups * slots if folds > 1 else slots, groups * pack), BF16),
            pltpu.VMEM((groups, groups * pack), F32),
            pltpu.VMEM((2, chunks, part, hf), BF16),
            pltpu.VMEM((2, chunks, part, hf), BF16),
            dma((6,)),
        ]
        + [dma((1,)) for _ in range(6)]
        + [dma((1,)), dma((groups // 2,)), dma((1,)), dma((1,))]
        + [dma((2,)), dma((2, 1 if chunks % reps == 0 else chunks))],
        compiler_params=pltpu.CompilerParams(
            collective_id=0, has_side_effects=True, vmem_limit_bytes=60 * 1024 * 1024
        ),
    )(
        image_len.reshape(groups, groups), image_order.reshape(1, groups), image_cut,
        qkv, embed_grad, out_weight,
    )
    emb, grad, wg = pl.pallas_call(
        write_out,
        out_shape=(
            jax.ShapeDtypeStruct((rows, width), BF16),
            jax.ShapeDtypeStruct((rows, feats3), BF16),
            jax.ShapeDtypeStruct((chunks, part, hf), F32),
        ),
        in_specs=[vmem, vmem, vmem],
        out_specs=(any_space, any_space, any_space),
        scratch_shapes=[dma((3,))],
    )(*(pltpu.with_memory_space_constraint(x, pltpu.VMEM) for x in (emb, grad, wg)))
    return emb, grad, wg.reshape(share, hf)


def solution(mesh):
    return jax.shard_map(
        functools.partial(local, mesh.shape["group"], mesh.shape["dp"]),
        mesh=mesh,
        in_specs=(
            P(("dp", "group"), None),
            P(("dp", "group"), None),
            P(),
            P("dp", None, None),
            P("dp", "group", None),
            P("dp", "group"),
        ),
        out_specs=(P(("dp", "group"), None), P(("dp", "group"), None), P("group", None)),
        check_vma=False,
    )
```

```python
import functools
import math

import jax
import jax.numpy as jnp
from jax import lax
from jax.experimental import pallas as pl
from jax.experimental.pallas import tpu as pltpu
from jax.sharding import PartitionSpec as P

HD = 80
HEADS = 8
SLOT = 8
MASKED = -1e30
F32 = jnp.float32
BF16 = jnp.bfloat16
MESH = pl.DeviceIdType.MESH


TRACE = False
CUT = 2
RS_ORDER = (0, 3, 2, 1)
open_scope = []


def mark(name):
    if TRACE:
        if open_scope:
            open_scope.pop().__exit__(None, None, None)
        if name:
            scope = jax.named_scope(name)
            scope.__enter__()
            open_scope.append(scope)


def dot(a, b, dims=((1,), (0,))):
    return lax.dot_general(a, b, (dims, ((), ())), preferred_element_type=F32)


TN = ((0,), (0,))
NT = ((1,), (1,))


def iota(shape, dim):
    return lax.broadcasted_iota(jnp.int32, shape, dim)


def flat(x):
    g, s, c = x.shape
    return x.astype(F32).reshape(g * s, c).astype(BF16)


def partner(me, k):
    out, bit = me, 1
    while bit <= k:
        if k & bit:
            has = lax.rem(lax.div(me, bit), 2)
            out = out + bit * (1 - 2 * has)
        bit *= 2
    return out


def kernel(
    groups, reps,
    len_hbm, order_hbm, cut_hbm, qkv_hbm, cot_hbm, w_hbm,
    emb, grad, own,
    len_ref, order_ref, cut_ref, qkv, cot, w, sel, pack_t,
    sendq, recvq, sendg, recvg, cots, cotr, qbig, gbig, attall,
    grads, backs, backr, cot_t, spread, slot_rows, zsend, zbuf,
    in_sem,
    sq, rq, sg, rg, sc, rc, sa, ra, sb, rb, sz, rz, known,
):
    me = lax.axis_index("group")
    rep = lax.axis_index("dp")
    rows, feats3 = qkv.shape
    hf = feats3 // 3
    width = cot.shape[1]
    slots = groups * SLOT
    pack = slots // 2
    every = groups * pack
    share = width // groups
    folds = share // cots.shape[1]
    chunks = zbuf.shape[1]

    mark("m00_start")
    barrier = pltpu.get_barrier_semaphore()
    blocked = chunks % reps == 0
    order_k = list(range(groups - 1, 0, -1))
    for k in order_k:
        pl.semaphore_signal(
            barrier, inc=1, device_id={"group": partner(me, k)}, device_id_type=MESH
        )

    peers = (rep > 0).astype(jnp.int32) + (rep < reps - 1).astype(jnp.int32)

    def greet(sem):
        @pl.when(rep > 0)
        def _():
            pl.semaphore_signal(sem, inc=1, device_id={"dp": rep - 1}, device_id_type=MESH)

        @pl.when(rep < reps - 1)
        def _():
            pl.semaphore_signal(sem, inc=1, device_id={"dp": rep + 1}, device_id_type=MESH)

    greet(barrier)

    loads = [
        pltpu.make_async_copy(src, dst, in_sem.at[i])
        for i, (src, dst) in enumerate(
            (
                (qkv_hbm, qkv), (cot_hbm, cot), (w_hbm, w),
                (len_hbm, len_ref), (order_hbm, order_ref), (cut_hbm, cut_ref),
            )
        )
    ]
    for i in (3, 4, 0, 1, 2, 5):
        loads[i].start()

    mark("m01_book")
    for i in (3, 4):
        loads[i].wait()
    sub = iota((groups, groups), 0)
    lane = iota((groups, groups), 1)
    eye = sub == lane
    lens = len_ref[...].astype(F32)
    lens_row = jnp.sum(jnp.where(sub == me, lens, 0.0), axis=0, keepdims=True)
    order_row = order_ref[...].astype(F32)
    order_col = jnp.sum(
        jnp.where(eye, jnp.broadcast_to(order_row, eye.shape), 0.0), axis=1, keepdims=True
    )
    onehot = jnp.where(order_col == lane.astype(F32), 1.0, 0.0)
    ordered_col = jnp.sum(onehot * lens_row, axis=1, keepdims=True)
    ordered_row = jnp.sum(jnp.where(eye, ordered_col, 0.0), axis=0, keepdims=True)
    starts_col = jnp.sum(
        jnp.where(lane < sub, jnp.broadcast_to(ordered_row, eye.shape), 0.0),
        axis=1, keepdims=True,
    )
    dest_row = jnp.sum(onehot * starts_col, axis=0, keepdims=True)
    block_of = iota((slots, groups), 0) // SLOT == iota((slots, groups), 1)
    within = lax.rem(iota((slots, 1), 0), SLOT).astype(F32)
    send_start = jnp.sum(jnp.where(block_of, dest_row, 0.0), axis=1, keepdims=True)
    send_len = jnp.sum(jnp.where(block_of, lens_row, 0.0), axis=1, keepdims=True)
    send_pos = jnp.where(within < send_len, send_start + within, -1.0)
    sel[...] = jnp.where(send_pos == iota((slots, rows), 1).astype(F32), 1.0, 0.0).astype(BF16)

    def remote(src, dst, ssem, rsem, k):
        return pltpu.make_async_remote_copy(
            src_ref=src, dst_ref=dst, send_sem=ssem, recv_sem=rsem,
            device_id={"group": partner(me, k)}, device_id_type=MESH,
        )

    def exchange(src, dst, ssem, rsem):
        for k in order_k:
            remote(src.at[partner(me, k)], dst.at[me], ssem, rsem, k).start()
        pltpu.make_async_copy(src.at[me], dst.at[me], rsem).start()

    def arrived(dst, ssem, rsem):
        remote(dst, dst, ssem, rsem, 1).wait_recv()

    def departed(src, ssem, rsem):
        most = src.at[pl.ds(0, groups - 1)]
        remote(most, most, ssem, rsem, 1).wait_send()

    mark("m02_selq")
    loads[0].wait()
    sendq[...] = dot(sel[...], qkv[...]).reshape(groups, SLOT, feats3).astype(BF16)

    mark("m03_barrier")
    pl.semaphore_wait(barrier, groups - 1 + peers)
    if blocked:
        greet(known.at[0])

    mark("m04_sendq")
    exchange(sendq, recvq, sq.at[0], rq.at[0])

    mark("m05_attgrad")
    loads[1].wait()
    loads[2].wait()
    att_grad = dot(cot[...], w[...]).astype(BF16)
    sendg[...] = dot(sel[...], att_grad).reshape(groups, SLOT, hf).astype(BF16)
    mark("m06_cot")
    turned = dot(cot[...], sel[...], ((0,), (1,))).reshape(groups, folds, share // folds, slots)
    cots[...] = jnp.concatenate([turned[:, f] for f in range(folds)], axis=2).astype(BF16)

    mark("m065_book2")
    before = jnp.where(lane < sub, 1.0, 0.0).astype(BF16)
    lens_b = lens.astype(BF16)
    starts = dot(before, lens_b)
    expand = jnp.where(block_of, 1.0, 0.0).astype(BF16)
    starts_me = jnp.sum(jnp.where(lane == me, starts, 0.0), axis=1, keepdims=True).astype(BF16)
    lens_me = jnp.sum(jnp.where(lane == me, lens, 0.0), axis=1, keepdims=True).astype(BF16)
    pos_me = dot(expand, jnp.broadcast_to(starts_me, (groups, pack))) + within
    held_me = within < dot(expand, jnp.broadcast_to(lens_me, (groups, pack)))
    packs = iota((slots, pack), 1).astype(F32)
    pack_t[...] = jnp.where((pos_me == packs) & held_me, 1.0, 0.0).astype(BF16)

    fill = iota((groups, every), 1) // pack == iota((groups, every), 0)
    fill = jnp.where(fill, 1.0, 0.0).astype(BF16)
    first_of = dot(starts.astype(BF16), fill)
    count_of = dot(lens_b, fill)
    place_of = lax.rem(iota((groups, every), 1), pack).astype(F32) - first_of
    place_of = jnp.where((place_of >= 0.0) & (place_of < count_of), place_of, -1.0)
    slot_of = jnp.where(
        place_of >= 0.0, place_of + (iota((groups, every), 1) // pack * SLOT).astype(F32), -1.0
    )
    slot_row = iota((slots, every), 0).astype(F32)
    if folds > 1:
        for s in range(groups):
            spread[s * slots : (s + 1) * slots, :] = jnp.where(
                slot_row == slot_of[s : s + 1, :], 1.0, 0.0
            ).astype(BF16)
    else:
        slot_rows[...] = slot_of
    mine = jnp.sum(
        jnp.where(iota((groups, every), 0) == me, slot_of, 0.0), axis=0, keepdims=True
    )
    home = dot(
        sel[...], jnp.where(slot_row == mine, 1.0, 0.0).astype(BF16), TN
    ).astype(BF16)

    departed(sendq, sq.at[0], rq.at[0])
    exchange(cots, cotr, sc.at[0], rc.at[0])

    mark("m07_waitq")
    arrived(recvq, sq.at[0], rq.at[0])
    if blocked:
        for i in range(1, reps - 2):
            pl.semaphore_wait(known.at[i - 1], peers)
            greet(known.at[i])
    mark("m08_att")
    loads[5].wait()
    xq = dot(pack_t[...], flat(recvq[...]), TN).astype(BF16)
    query, keys, values = xq[:, :hf], xq[:, hf : 2 * hf], xq[:, 2 * hf :]
    feature = iota((1, hf), 1)
    heads = [
        (feature >= h * HD) & (feature < (h + 1) * HD) for h in range(HEADS)
    ]
    marks = [jnp.where(m, 1.0, 0.0).astype(BF16) for m in heads]
    for h in range(HEADS):
        qbig[h * pack : (h + 1) * pack, :] = query * marks[h]
    scale = 1.0 / math.sqrt(HD)
    cut = cut_ref[...]
    wide = HEADS * pack
    row_second = iota((pack, wide), 0) >= cut
    col_second = lax.rem(iota((pack, wide), 1), pack) >= cut
    same = row_second == col_second
    scores = dot(keys, qbig[...], NT) * scale
    scores = jnp.where(same, scores, MASKED)
    top = jnp.max(scores, axis=0, keepdims=True)
    expo = jnp.exp(scores - top)
    probs = expo / jnp.sum(expo, axis=0, keepdims=True)
    probs_b = probs.astype(BF16)

    def per_head(big):
        out = jnp.where(heads[0], big[:pack], 0.0)
        for h in range(1, HEADS):
            out = jnp.where(heads[h], big[h * pack : (h + 1) * pack], out)
        return out.astype(BF16)

    att = per_head(dot(probs_b, values, TN))
    attall[pl.ds(me, 1)] = att.reshape(1, pack, hf)
    direct = list(range(groups - 2, 0, -2))
    for k in direct:
        remote(attall.at[me], attall.at[me], sa.at[0], ra.at[k // 2], k).start()
    remote(attall.at[me], attall.at[me], sa.at[0], ra.at[0], 1).start()


    mark("m11_waitc")
    arrived(cotr, sc.at[0], rc.at[0])
    mark("m12_pack")
    if folds > 1:
        pieces = [cotr[s].astype(F32) for s in range(groups)]
        left = jnp.concatenate(
            [
                jnp.concatenate(
                    [piece[:, f * slots : (f + 1) * slots] for piece in pieces], axis=1
                )
                for f in range(folds)
            ],
            axis=0,
        ).astype(BF16)
        cot_t[...] = dot(left, spread[...]).astype(BF16)
    else:
        cot_t[...] = jnp.zeros(cot_t.shape, BF16)

        def place(s, carry):
            spread[...] = jnp.where(
                slot_row == slot_rows[pl.ds(s, 1), :], 1.0, 0.0
            ).astype(BF16)
            cot_t[...] = cot_t[...] + dot(cotr[s], spread[...]).astype(BF16)
            return carry

        lax.fori_loop(0, groups, place, 0)

    mark("m13_waita")
    for k in direct[::-1]:
        remote(attall.at[me], attall.at[me], sa.at[0], ra.at[k // 2], k).wait_recv()
        piece = attall.at[partner(me, k)]
        remote(piece, piece, sa.at[0], ra.at[0], 1).start()
    exchange(sendg, recvg, sg.at[0], rg.at[0])
    half = attall.at[pl.ds(0, groups // 2)]
    remote(half, half, sa.at[0], ra.at[0], 1).wait_recv()
    mark("m14_wg")
    att_rows = attall[...].reshape(every, hf)
    own[...] = dot(cot_t[...], att_rows).reshape(own.shape)

    def backward():
        mark("m09_waitg")
        arrived(recvg, sg.at[0], rg.at[0])
        mark("m10_bwd")
        xg = dot(pack_t[...], flat(recvg[...]), TN).astype(BF16)
        for h in range(HEADS):
            gbig[h * pack : (h + 1) * pack, :] = xg * marks[h]
        prob_grad = dot(values, gbig[...], NT)
        delta = jnp.sum(probs * prob_grad, axis=0, keepdims=True)
        score_grad = (probs * (prob_grad - delta) * scale).astype(BF16)
        grads[:, :hf] = per_head(dot(score_grad, keys, TN))
        grads[:, hf : 2 * hf] = dot(score_grad, qbig[...]).astype(BF16)
        grads[:, 2 * hf :] = dot(probs_b, gbig[...]).astype(BF16)

        backs[...] = dot(pack_t[...], grads[...]).reshape(groups, SLOT, feats3).astype(BF16)
        exchange(backs, backr, sb.at[0], rb.at[0])


    def project():
        mark("m16_emb")
        emb[...] = dot(dot(home, att_rows).astype(BF16), w[...], NT).astype(BF16)

    def source_rows():
        mark("m17_waitb")
        arrived(backr, sb.at[0], rb.at[0])
        mark("m18_back")
        grad[...] = dot(sel[...], flat(backr[...]), TN).astype(BF16)
        mark("m19_z")

    def along_line():
        mark("m15_zchain")
        @pl.when(rep == 0)
        def _():
            zbuf[0] = jnp.zeros(zbuf.shape[1:], BF16)

        @pl.when(rep == reps - 1)
        def _():
            zbuf[1] = jnp.zeros(zbuf.shape[1:], BF16)

        def hop(way, c):
            return pltpu.make_async_remote_copy(
                src_ref=zsend.at[way, c], dst_ref=zbuf.at[way, c],
                send_sem=sz.at[way], recv_sem=rz.at[way, c],
                device_id={"dp": rep + 1 - 2 * way}, device_id_type=MESH,
            )

        def step(way, c):
            spot = rep + way * (reps - 1 - 2 * rep)

            @pl.when(spot > 0)
            def _():
                hop(way, c).wait_recv()

            @pl.when(spot < reps - 1)
            def _():
                zsend[way, c] = (own[c] + zbuf[way, c].astype(F32)).astype(BF16)
                hop(way, c).start()

        near = (rep >= (reps + 1) // 2).astype(jnp.int32)
        edge = (rep == 0) | (rep == reps - 1)

        @pl.when(edge)
        def _():
            for c in range(chunks):
                step(near, c)

        backward()
        project()

        @pl.when(edge)
        def _():
            source_rows()
            for c in range(chunks):
                step(1 - near, c)

        @pl.when(jnp.logical_not(edge))
        def _():
            mark("m19_zmid")
            lag = chunks // 2
            for t in range(chunks + lag):
                if t < chunks:
                    step(near, t)
                if t >= lag:
                    step(1 - near, t - lag)
            source_rows()

        mark("m20_final")
        own[...] = own[...] + zbuf[0].astype(F32) + zbuf[1].astype(F32)

        for way in range(2):
            spot = rep + way * (reps - 1 - 2 * rep)

            @pl.when(spot < reps - 1)
            def _():
                pltpu.make_async_remote_copy(
                    src_ref=zsend.at[way], dst_ref=zbuf.at[way],
                    send_sem=sz.at[way], recv_sem=rz.at[way, 0],
                    device_id={"dp": rep + 1 - 2 * way}, device_id_type=MESH,
                ).wait_send()


    def by_blocks():
        size = chunks // reps
        cuts = [0, CUT, size] if size > CUT else [0, size]
        spans = list(zip(cuts[:-1], cuts[1:]))
        rounds = len(spans)

        def across(src, dst, i, to):
            return pltpu.make_async_remote_copy(
                src_ref=src, dst_ref=dst, send_sem=sz.at[i], recv_sem=rz.at[i, 0],
                device_id={"dp": to}, device_id_type=MESH,
            )

        mark("m15_scatter")
        pl.semaphore_wait(known.at[reps - 3], peers)
        zsend[0] = own[...].astype(BF16)
        for i, (low, high) in enumerate(spans):
            for to in RS_ORDER:

                @pl.when(rep != to)
                def _():
                    across(
                        zsend.at[0, pl.ds(to * size + low, high - low)],
                        zbuf.at[0, pl.ds(low * reps + rep * (high - low), high - low)],
                        i, to,
                    ).start()

        backward()
        project()
        for i, (low, high) in enumerate(spans):
            wide = high - low
            mark(f"m17_waits{i}")
            most = zbuf.at[0, pl.ds(0, wide * (reps - 1))]
            across(most, most, i, rep).wait_recv()
            mark(f"m18_sum{i}")
            mine = pl.ds(rep * size + low, wide)
            zbuf[0, pl.ds(low * reps + rep * wide, wide)] = jnp.zeros(
                (wide,) + zbuf.shape[2:], BF16
            )
            total = own[mine]
            for r in range(reps):
                first = low * reps + r * wide
                total = total + zbuf[0, first : first + wide].astype(F32)
            zbuf[1, mine] = total.astype(BF16)
            for to in range(reps):

                @pl.when(rep != to)
                def _():
                    across(zbuf.at[1, mine], zbuf.at[1, mine], rounds + i, to).start()

        source_rows()
        for i, (low, high) in enumerate(spans):
            most = zbuf.at[0, pl.ds(0, (high - low) * (reps - 1))]
            across(most, most, rounds + i, rep).wait_recv()
        mark("m20_final")
        own[...] = zbuf[1].astype(F32)
        for i in range(2 * rounds):
            low, high = spans[i % rounds]
            most = zbuf.at[0, pl.ds(0, (high - low) * (reps - 1))]
            across(most, most, i, rep).wait_send()

    if blocked:
        by_blocks()
    else:
        along_line()

    mark("m21_drain")
    departed(sendg, sg.at[0], rg.at[0])
    departed(cots, sc.at[0], rc.at[0])
    departed(backs, sb.at[0], rb.at[0])
    departed(attall, sa.at[0], ra.at[0])
    mark(None)


def write_out(emb, grad, own, emb_hbm, grad_hbm, wg_hbm, sems):
    pairs = ((emb, emb_hbm), (grad, grad_hbm), (own, wg_hbm))
    copies = [
        pltpu.make_async_copy(src, dst, sems.at[i]) for i, (src, dst) in enumerate(pairs)
    ]
    for copy in copies:
        copy.start()
    for copy in copies:
        copy.wait()


def local(groups, reps, qkv, embed_grad, out_weight, image_len, image_order, image_cut):
    rows, feats3 = qkv.shape
    width, hf = out_weight.shape
    slots = groups * SLOT
    pack = slots // 2
    share = width // groups
    part = 8 if share % (8 * reps) == 0 or share % 16 else 16
    chunks = share // part
    folds = 2 if slots < 128 and share % 32 == 0 else 1
    any_space = pl.BlockSpec(memory_space=pl.ANY)
    vmem = pl.BlockSpec(memory_space=pltpu.VMEM)
    dma = pltpu.SemaphoreType.DMA
    emb, grad, wg = pl.pallas_call(
        functools.partial(kernel, groups, reps),
        out_shape=(
            pltpu.VMEM((rows, width), BF16),
            pltpu.VMEM((rows, feats3), BF16),
            pltpu.VMEM((chunks, part, hf), F32),
        ),
        in_specs=[any_space] * 6,
        out_specs=(vmem, vmem, vmem),
        scratch_shapes=[
            pltpu.VMEM((groups, groups), jnp.int32),
            pltpu.VMEM((1, groups), jnp.int32),
            pltpu.VMEM((1, 1), jnp.int32),
            pltpu.VMEM((rows, feats3), BF16),
            pltpu.VMEM((rows, width), BF16),
            pltpu.VMEM((width, hf), BF16),
            pltpu.VMEM((slots, rows), BF16),
            pltpu.VMEM((slots, pack), BF16),
            pltpu.VMEM((groups, SLOT, feats3), BF16),
            pltpu.VMEM((groups, SLOT, feats3), BF16),
            pltpu.VMEM((groups, SLOT, hf), BF16),
            pltpu.VMEM((groups, SLOT, hf), BF16),
            pltpu.VMEM((groups, share // folds, slots * folds), BF16),
            pltpu.VMEM((groups, share // folds, slots * folds), BF16),
            pltpu.VMEM((HEADS * pack, hf), BF16),
            pltpu.VMEM((HEADS * pack, hf), BF16),
            pltpu.VMEM((groups, pack, hf), BF16),
            pltpu.VMEM((pack, feats3), BF16),
            pltpu.VMEM((groups, SLOT, feats3), BF16),
            pltpu.VMEM((groups, SLOT, feats3), BF16),
            pltpu.VMEM((share, groups * pack), BF16),
            pltpu.VMEM((groups * slots if folds > 1 else slots, groups * pack), BF16),
            pltpu.VMEM((groups, groups * pack), F32),
            pltpu.VMEM((2, chunks, part, hf), BF16),
            pltpu.VMEM((2, chunks, part, hf), BF16),
            dma((6,)),
        ]
        + [dma((1,)) for _ in range(6)]
        + [dma((1,)), dma((groups // 2,)), dma((1,)), dma((1,))]
        + ([dma((4,)), dma((4, 1))] if chunks % reps == 0 else [dma((2,)), dma((2, chunks))])
        + [pltpu.SemaphoreType.REGULAR((max(reps - 2, 1),))],
        compiler_params=pltpu.CompilerParams(
            collective_id=0, has_side_effects=True, vmem_limit_bytes=60 * 1024 * 1024
        ),
    )(
        image_len.reshape(groups, groups), image_order.reshape(1, groups), image_cut,
        qkv, embed_grad, out_weight,
    )
    emb, grad, wg = pl.pallas_call(
        write_out,
        out_shape=(
            jax.ShapeDtypeStruct((rows, width), BF16),
            jax.ShapeDtypeStruct((rows, feats3), BF16),
            jax.ShapeDtypeStruct((chunks, part, hf), F32),
        ),
        in_specs=[vmem, vmem, vmem],
        out_specs=(any_space, any_space, any_space),
        scratch_shapes=[dma((3,))],
    )(*(pltpu.with_memory_space_constraint(x, pltpu.VMEM) for x in (emb, grad, wg)))
    return emb, grad, wg.reshape(share, hf)


def solution(mesh):
    return jax.shard_map(
        functools.partial(local, mesh.shape["group"], mesh.shape["dp"]),
        mesh=mesh,
        in_specs=(
            P(("dp", "group"), None),
            P(("dp", "group"), None),
            P(),
            P("dp", None, None),
            P("dp", "group", None),
            P("dp", "group"),
        ),
        out_specs=(P(("dp", "group"), None), P(("dp", "group"), None), P("group", None)),
        check_vma=False,
    )
```

```python
import functools
import math

import jax
import jax.numpy as jnp
from jax import lax
from jax.experimental import pallas as pl
from jax.experimental.pallas import tpu as pltpu
from jax.sharding import PartitionSpec as P

HD = 80
HEADS = 8
SLOT = 8
MASKED = -1e30
F32 = jnp.float32
BF16 = jnp.bfloat16
MESH = pl.DeviceIdType.MESH


TRACE = False
CUT = 2
RS_ORDER = (0, 3, 2, 1)
open_scope = []


def mark(name):
    if TRACE:
        if open_scope:
            open_scope.pop().__exit__(None, None, None)
        if name:
            scope = jax.named_scope(name)
            scope.__enter__()
            open_scope.append(scope)


def dot(a, b, dims=((1,), (0,))):
    return lax.dot_general(a, b, (dims, ((), ())), preferred_element_type=F32)


TN = ((0,), (0,))
NT = ((1,), (1,))


def iota(shape, dim):
    return lax.broadcasted_iota(jnp.int32, shape, dim)


def flat(x):
    g, s, c = x.shape
    return x.astype(F32).reshape(g * s, c).astype(BF16)


def partner(me, k):
    out, bit = me, 1
    while bit <= k:
        if k & bit:
            has = lax.rem(lax.div(me, bit), 2)
            out = out + bit * (1 - 2 * has)
        bit *= 2
    return out


def kernel(
    groups, reps,
    len_hbm, order_hbm, cut_hbm, qkv_hbm, cot_hbm, w_hbm,
    emb, grad, own,
    len_ref, order_ref, cut_ref, qkv, cot, w, sel, pack_t,
    sendq, recvq, sendg, recvg, cots, cotr, qbig, gbig, attall,
    grads, backs, backr, cot_t, spread, slot_rows, zsend, zbuf,
    in_sem,
    sq, rq, sg, rg, sc, rc, sa, ra, sb, rb, sz, rz, known,
):
    me = lax.axis_index("group")
    rep = lax.axis_index("dp")
    rows, feats3 = qkv.shape
    hf = feats3 // 3
    width = cot.shape[1]
    slots = groups * SLOT
    pack = slots // 2
    every = groups * pack
    share = width // groups
    folds = share // cots.shape[1]
    chunks = zbuf.shape[1]

    mark("m00_start")
    barrier = pltpu.get_barrier_semaphore()
    blocked = chunks % reps == 0
    order_k = list(range(groups - 1, 0, -1))
    for k in order_k:
        pl.semaphore_signal(
            barrier, inc=1, device_id={"group": partner(me, k)}, device_id_type=MESH
        )

    peers = (rep > 0).astype(jnp.int32) + (rep < reps - 1).astype(jnp.int32)

    def greet(sem):
        @pl.when(rep > 0)
        def _():
            pl.semaphore_signal(sem, inc=1, device_id={"dp": rep - 1}, device_id_type=MESH)

        @pl.when(rep < reps - 1)
        def _():
            pl.semaphore_signal(sem, inc=1, device_id={"dp": rep + 1}, device_id_type=MESH)

    greet(barrier)

    loads = [
        pltpu.make_async_copy(src, dst, in_sem.at[i])
        for i, (src, dst) in enumerate(
            (
                (qkv_hbm, qkv), (cot_hbm, cot), (w_hbm, w),
                (len_hbm, len_ref), (order_hbm, order_ref), (cut_hbm, cut_ref),
            )
        )
    ]
    for i in (3, 4, 0, 1, 2, 5):
        loads[i].start()

    mark("m01_book")
    for i in (3, 4):
        loads[i].wait()
    sub = iota((groups, groups), 0)
    lane = iota((groups, groups), 1)
    eye = sub == lane
    lens = len_ref[...].astype(F32)
    lens_row = jnp.sum(jnp.where(sub == me, lens, 0.0), axis=0, keepdims=True)
    order_row = order_ref[...].astype(F32)
    order_col = jnp.sum(
        jnp.where(eye, jnp.broadcast_to(order_row, eye.shape), 0.0), axis=1, keepdims=True
    )
    onehot = jnp.where(order_col == lane.astype(F32), 1.0, 0.0)
    ordered_col = jnp.sum(onehot * lens_row, axis=1, keepdims=True)
    ordered_row = jnp.sum(jnp.where(eye, ordered_col, 0.0), axis=0, keepdims=True)
    starts_col = jnp.sum(
        jnp.where(lane < sub, jnp.broadcast_to(ordered_row, eye.shape), 0.0),
        axis=1, keepdims=True,
    )
    dest_row = jnp.sum(onehot * starts_col, axis=0, keepdims=True)
    block_of = iota((slots, groups), 0) // SLOT == iota((slots, groups), 1)
    within = lax.rem(iota((slots, 1), 0), SLOT).astype(F32)
    send_start = jnp.sum(jnp.where(block_of, dest_row, 0.0), axis=1, keepdims=True)
    send_len = jnp.sum(jnp.where(block_of, lens_row, 0.0), axis=1, keepdims=True)
    send_pos = jnp.where(within < send_len, send_start + within, -1.0)
    sel[...] = jnp.where(send_pos == iota((slots, rows), 1).astype(F32), 1.0, 0.0).astype(BF16)

    def remote(src, dst, ssem, rsem, k):
        return pltpu.make_async_remote_copy(
            src_ref=src, dst_ref=dst, send_sem=ssem, recv_sem=rsem,
            device_id={"group": partner(me, k)}, device_id_type=MESH,
        )

    def exchange(src, dst, ssem, rsem):
        for k in order_k:
            remote(src.at[partner(me, k)], dst.at[me], ssem, rsem, k).start()
        pltpu.make_async_copy(src.at[me], dst.at[me], rsem).start()

    def arrived(dst, ssem, rsem):
        remote(dst, dst, ssem, rsem, 1).wait_recv()

    def departed(src, ssem, rsem):
        most = src.at[pl.ds(0, groups - 1)]
        remote(most, most, ssem, rsem, 1).wait_send()

    mark("m02_selq")
    loads[0].wait()
    sendq[...] = dot(sel[...], qkv[...]).reshape(groups, SLOT, feats3).astype(BF16)

    mark("m03_barrier")
    pl.semaphore_wait(barrier, groups - 1 + peers)
    if blocked:
        greet(known.at[0])

    mark("m04_sendq")
    exchange(sendq, recvq, sq.at[0], rq.at[0])

    mark("m05_attgrad")
    loads[1].wait()
    loads[2].wait()
    att_grad = dot(cot[...], w[...]).astype(BF16)
    sendg[...] = dot(sel[...], att_grad).reshape(groups, SLOT, hf).astype(BF16)
    mark("m06_cot")
    turned = dot(cot[...], sel[...], ((0,), (1,))).reshape(groups, folds, share // folds, slots)
    cots[...] = jnp.concatenate([turned[:, f] for f in range(folds)], axis=2).astype(BF16)

    mark("m065_book2")
    before = jnp.where(lane < sub, 1.0, 0.0).astype(BF16)
    lens_b = lens.astype(BF16)
    starts = dot(before, lens_b)
    expand = jnp.where(block_of, 1.0, 0.0).astype(BF16)
    starts_me = jnp.sum(jnp.where(lane == me, starts, 0.0), axis=1, keepdims=True).astype(BF16)
    lens_me = jnp.sum(jnp.where(lane == me, lens, 0.0), axis=1, keepdims=True).astype(BF16)
    pos_me = dot(expand, jnp.broadcast_to(starts_me, (groups, pack))) + within
    held_me = within < dot(expand, jnp.broadcast_to(lens_me, (groups, pack)))
    packs = iota((slots, pack), 1).astype(F32)
    pack_t[...] = jnp.where((pos_me == packs) & held_me, 1.0, 0.0).astype(BF16)

    fill = iota((groups, every), 1) // pack == iota((groups, every), 0)
    fill = jnp.where(fill, 1.0, 0.0).astype(BF16)
    first_of = dot(starts.astype(BF16), fill)
    count_of = dot(lens_b, fill)
    place_of = lax.rem(iota((groups, every), 1), pack).astype(F32) - first_of
    place_of = jnp.where((place_of >= 0.0) & (place_of < count_of), place_of, -1.0)
    slot_of = jnp.where(
        place_of >= 0.0, place_of + (iota((groups, every), 1) // pack * SLOT).astype(F32), -1.0
    )
    slot_row = iota((slots, every), 0).astype(F32)
    if folds > 1:
        for s in range(groups):
            spread[s * slots : (s + 1) * slots, :] = jnp.where(
                slot_row == slot_of[s : s + 1, :], 1.0, 0.0
            ).astype(BF16)
    else:
        slot_rows[...] = slot_of
    mine = jnp.sum(
        jnp.where(iota((groups, every), 0) == me, slot_of, 0.0), axis=0, keepdims=True
    )
    home = dot(
        sel[...], jnp.where(slot_row == mine, 1.0, 0.0).astype(BF16), TN
    ).astype(BF16)

    departed(sendq, sq.at[0], rq.at[0])
    exchange(cots, cotr, sc.at[0], rc.at[0])

    mark("m07_waitq")
    arrived(recvq, sq.at[0], rq.at[0])
    if blocked:
        for i in range(1, reps - 2):
            pl.semaphore_wait(known.at[i - 1], peers)
            greet(known.at[i])
    mark("m08_att")
    loads[5].wait()
    xq = dot(pack_t[...], flat(recvq[...]), TN).astype(BF16)
    query, keys, values = xq[:, :hf], xq[:, hf : 2 * hf], xq[:, 2 * hf :]
    feature = iota((1, hf), 1)
    heads = [
        (feature >= h * HD) & (feature < (h + 1) * HD) for h in range(HEADS)
    ]
    marks = [jnp.where(m, 1.0, 0.0).astype(BF16) for m in heads]
    for h in range(HEADS):
        qbig[h * pack : (h + 1) * pack, :] = query * marks[h]
    scale = 1.0 / math.sqrt(HD)
    cut = cut_ref[...]
    wide = HEADS * pack
    row_second = iota((pack, wide), 0) >= cut
    col_second = lax.rem(iota((pack, wide), 1), pack) >= cut
    same = row_second == col_second
    scores = dot(keys, qbig[...], NT) * scale
    scores = jnp.where(same, scores, MASKED)
    top = jnp.max(scores, axis=0, keepdims=True)
    expo = jnp.exp(scores - top)
    probs = expo / jnp.sum(expo, axis=0, keepdims=True)
    probs_b = probs.astype(BF16)

    def per_head(big):
        out = jnp.where(heads[0], big[:pack], 0.0)
        for h in range(1, HEADS):
            out = jnp.where(heads[h], big[h * pack : (h + 1) * pack], out)
        return out.astype(BF16)

    att = per_head(dot(probs_b, values, TN))
    attall[pl.ds(me, 1)] = att.reshape(1, pack, hf)
    direct = list(range(groups - 2, 0, -2))
    for k in direct:
        remote(attall.at[me], attall.at[me], sa.at[0], ra.at[k // 2], k).start()
    remote(attall.at[me], attall.at[me], sa.at[0], ra.at[0], 1).start()


    mark("m11_waitc")
    arrived(cotr, sc.at[0], rc.at[0])
    mark("m12_pack")
    if folds > 1:
        pieces = [cotr[s].astype(F32) for s in range(groups)]
        left = jnp.concatenate(
            [
                jnp.concatenate(
                    [piece[:, f * slots : (f + 1) * slots] for piece in pieces], axis=1
                )
                for f in range(folds)
            ],
            axis=0,
        ).astype(BF16)
        cot_t[...] = dot(left, spread[...]).astype(BF16)
    else:
        cot_t[...] = jnp.zeros(cot_t.shape, BF16)

        def place(s, carry):
            spread[...] = jnp.where(
                slot_row == slot_rows[pl.ds(s, 1), :], 1.0, 0.0
            ).astype(BF16)
            cot_t[...] = cot_t[...] + dot(cotr[s], spread[...]).astype(BF16)
            return carry

        lax.fori_loop(0, groups, place, 0)

    mark("m13_waita")
    for k in direct[::-1]:
        remote(attall.at[me], attall.at[me], sa.at[0], ra.at[k // 2], k).wait_recv()
        piece = attall.at[partner(me, k)]
        remote(piece, piece, sa.at[0], ra.at[0], 1).start()
    exchange(sendg, recvg, sg.at[0], rg.at[0])
    half = attall.at[pl.ds(0, groups // 2)]
    remote(half, half, sa.at[0], ra.at[0], 1).wait_recv()
    mark("m14_wg")
    att_rows = attall[...].reshape(every, hf)
    own[...] = dot(cot_t[...], att_rows).reshape(own.shape)

    def backward():
        mark("m09_waitg")
        arrived(recvg, sg.at[0], rg.at[0])
        mark("m10_bwd")
        xg = dot(pack_t[...], flat(recvg[...]), TN).astype(BF16)
        for h in range(HEADS):
            gbig[h * pack : (h + 1) * pack, :] = xg * marks[h]
        prob_grad = dot(values, gbig[...], NT)
        delta = jnp.sum(probs * prob_grad, axis=0, keepdims=True)
        score_grad = (probs * (prob_grad - delta) * scale).astype(BF16)
        grads[:, :hf] = per_head(dot(score_grad, keys, TN))
        grads[:, hf : 2 * hf] = dot(score_grad, qbig[...]).astype(BF16)
        grads[:, 2 * hf :] = dot(probs_b, gbig[...]).astype(BF16)

        backs[...] = dot(pack_t[...], grads[...]).reshape(groups, SLOT, feats3).astype(BF16)
        exchange(backs, backr, sb.at[0], rb.at[0])


    def project():
        mark("m16_emb")
        emb[...] = dot(dot(home, att_rows).astype(BF16), w[...], NT).astype(BF16)

    def source_rows():
        mark("m17_waitb")
        arrived(backr, sb.at[0], rb.at[0])
        mark("m18_back")
        grad[...] = dot(sel[...], flat(backr[...]), TN).astype(BF16)
        mark("m19_z")

    def along_line():
        mark("m15_zchain")
        @pl.when(rep == 0)
        def _():
            zbuf[0] = jnp.zeros(zbuf.shape[1:], BF16)

        @pl.when(rep == reps - 1)
        def _():
            zbuf[1] = jnp.zeros(zbuf.shape[1:], BF16)

        def hop(way, c):
            return pltpu.make_async_remote_copy(
                src_ref=zsend.at[way, c], dst_ref=zbuf.at[way, c],
                send_sem=sz.at[way], recv_sem=rz.at[way, c],
                device_id={"dp": rep + 1 - 2 * way}, device_id_type=MESH,
            )

        def step(way, c):
            spot = rep + way * (reps - 1 - 2 * rep)

            @pl.when(spot > 0)
            def _():
                hop(way, c).wait_recv()

            @pl.when(spot < reps - 1)
            def _():
                zsend[way, c] = (own[c] + zbuf[way, c].astype(F32)).astype(BF16)
                hop(way, c).start()

        near = (rep >= (reps + 1) // 2).astype(jnp.int32)
        edge = (rep == 0) | (rep == reps - 1)

        @pl.when(edge)
        def _():
            for c in range(chunks):
                step(near, c)

        backward()
        project()

        @pl.when(edge)
        def _():
            source_rows()
            for c in range(chunks):
                step(1 - near, c)

        @pl.when(jnp.logical_not(edge))
        def _():
            mark("m19_zmid")
            lag = chunks // 2
            for t in range(chunks + lag):
                if t < chunks:
                    step(near, t)
                if t >= lag:
                    step(1 - near, t - lag)
            source_rows()

        mark("m20_final")
        own[...] = own[...] + zbuf[0].astype(F32) + zbuf[1].astype(F32)

        for way in range(2):
            spot = rep + way * (reps - 1 - 2 * rep)

            @pl.when(spot < reps - 1)
            def _():
                pltpu.make_async_remote_copy(
                    src_ref=zsend.at[way], dst_ref=zbuf.at[way],
                    send_sem=sz.at[way], recv_sem=rz.at[way, 0],
                    device_id={"dp": rep + 1 - 2 * way}, device_id_type=MESH,
                ).wait_send()


    def by_blocks():
        size = chunks // reps
        cuts = [0, CUT, size] if size > CUT else [0, size]
        spans = list(zip(cuts[:-1], cuts[1:]))
        rounds = len(spans)

        def across(src, dst, i, to):
            return pltpu.make_async_remote_copy(
                src_ref=src, dst_ref=dst, send_sem=sz.at[i], recv_sem=rz.at[i, 0],
                device_id={"dp": to}, device_id_type=MESH,
            )

        mark("m15_scatter")
        pl.semaphore_wait(known.at[reps - 3], peers)
        zsend[0] = own[...].astype(BF16)
        for i, (low, high) in enumerate(spans):
            for to in RS_ORDER:

                @pl.when(rep != to)
                def _():
                    across(
                        zsend.at[0, pl.ds(to * size + low, high - low)],
                        zbuf.at[0, pl.ds(low * reps + rep * (high - low), high - low)],
                        i, to,
                    ).start()

        project()
        for i, (low, high) in enumerate(spans):
            wide = high - low
            mark(f"m17_waits{i}")
            most = zbuf.at[0, pl.ds(0, wide * (reps - 1))]
            across(most, most, i, rep).wait_recv()
            mark(f"m18_sum{i}")
            mine = pl.ds(rep * size + low, wide)
            zbuf[0, pl.ds(low * reps + rep * wide, wide)] = jnp.zeros(
                (wide,) + zbuf.shape[2:], BF16
            )
            total = own[mine]
            for r in range(reps):
                first = low * reps + r * wide
                total = total + zbuf[0, first : first + wide].astype(F32)
            zbuf[1, mine] = total.astype(BF16)
            for to in range(reps):

                @pl.when(rep != to)
                def _():
                    across(zbuf.at[1, mine], zbuf.at[1, mine], rounds + i, to).start()
            if i == 0:
                backward()

        source_rows()
        for i, (low, high) in enumerate(spans):
            most = zbuf.at[0, pl.ds(0, (high - low) * (reps - 1))]
            across(most, most, rounds + i, rep).wait_recv()
        mark("m20_final")
        own[...] = zbuf[1].astype(F32)
        for i in range(2 * rounds):
            low, high = spans[i % rounds]
            most = zbuf.at[0, pl.ds(0, (high - low) * (reps - 1))]
            across(most, most, i, rep).wait_send()

    if blocked:
        by_blocks()
    else:
        along_line()

    mark("m21_drain")
    departed(sendg, sg.at[0], rg.at[0])
    departed(cots, sc.at[0], rc.at[0])
    departed(backs, sb.at[0], rb.at[0])
    departed(attall, sa.at[0], ra.at[0])
    mark(None)


def write_out(emb, grad, own, emb_hbm, grad_hbm, wg_hbm, sems):
    pairs = ((emb, emb_hbm), (grad, grad_hbm), (own, wg_hbm))
    copies = [
        pltpu.make_async_copy(src, dst, sems.at[i]) for i, (src, dst) in enumerate(pairs)
    ]
    for copy in copies:
        copy.start()
    for copy in copies:
        copy.wait()


def local(groups, reps, qkv, embed_grad, out_weight, image_len, image_order, image_cut):
    rows, feats3 = qkv.shape
    width, hf = out_weight.shape
    slots = groups * SLOT
    pack = slots // 2
    share = width // groups
    part = 8 if share % (8 * reps) == 0 or share % 16 else 16
    chunks = share // part
    folds = 2 if slots < 128 and share % 32 == 0 else 1
    any_space = pl.BlockSpec(memory_space=pl.ANY)
    vmem = pl.BlockSpec(memory_space=pltpu.VMEM)
    dma = pltpu.SemaphoreType.DMA
    emb, grad, wg = pl.pallas_call(
        functools.partial(kernel, groups, reps),
        out_shape=(
            pltpu.VMEM((rows, width), BF16),
            pltpu.VMEM((rows, feats3), BF16),
            pltpu.VMEM((chunks, part, hf), F32),
        ),
        in_specs=[any_space] * 6,
        out_specs=(vmem, vmem, vmem),
        scratch_shapes=[
            pltpu.VMEM((groups, groups), jnp.int32),
            pltpu.VMEM((1, groups), jnp.int32),
            pltpu.VMEM((1, 1), jnp.int32),
            pltpu.VMEM((rows, feats3), BF16),
            pltpu.VMEM((rows, width), BF16),
            pltpu.VMEM((width, hf), BF16),
            pltpu.VMEM((slots, rows), BF16),
            pltpu.VMEM((slots, pack), BF16),
            pltpu.VMEM((groups, SLOT, feats3), BF16),
            pltpu.VMEM((groups, SLOT, feats3), BF16),
            pltpu.VMEM((groups, SLOT, hf), BF16),
            pltpu.VMEM((groups, SLOT, hf), BF16),
            pltpu.VMEM((groups, share // folds, slots * folds), BF16),
            pltpu.VMEM((groups, share // folds, slots * folds), BF16),
            pltpu.VMEM((HEADS * pack, hf), BF16),
            pltpu.VMEM((HEADS * pack, hf), BF16),
            pltpu.VMEM((groups, pack, hf), BF16),
            pltpu.VMEM((pack, feats3), BF16),
            pltpu.VMEM((groups, SLOT, feats3), BF16),
            pltpu.VMEM((groups, SLOT, feats3), BF16),
            pltpu.VMEM((share, groups * pack), BF16),
            pltpu.VMEM((groups * slots if folds > 1 else slots, groups * pack), BF16),
            pltpu.VMEM((groups, groups * pack), F32),
            pltpu.VMEM((2, chunks, part, hf), BF16),
            pltpu.VMEM((2, chunks, part, hf), BF16),
            dma((6,)),
        ]
        + [dma((1,)) for _ in range(6)]
        + [dma((1,)), dma((groups // 2,)), dma((1,)), dma((1,))]
        + ([dma((4,)), dma((4, 1))] if chunks % reps == 0 else [dma((2,)), dma((2, chunks))])
        + [pltpu.SemaphoreType.REGULAR((max(reps - 2, 1),))],
        compiler_params=pltpu.CompilerParams(
            collective_id=0, has_side_effects=True, vmem_limit_bytes=60 * 1024 * 1024
        ),
    )(
        image_len.reshape(groups, groups), image_order.reshape(1, groups), image_cut,
        qkv, embed_grad, out_weight,
    )
    emb, grad, wg = pl.pallas_call(
        write_out,
        out_shape=(
            jax.ShapeDtypeStruct((rows, width), BF16),
            jax.ShapeDtypeStruct((rows, feats3), BF16),
            jax.ShapeDtypeStruct((chunks, part, hf), F32),
        ),
        in_specs=[vmem, vmem, vmem],
        out_specs=(any_space, any_space, any_space),
        scratch_shapes=[dma((3,))],
    )(*(pltpu.with_memory_space_constraint(x, pltpu.VMEM) for x in (emb, grad, wg)))
    return emb, grad, wg.reshape(share, hf)


def solution(mesh):
    return jax.shard_map(
        functools.partial(local, mesh.shape["group"], mesh.shape["dp"]),
        mesh=mesh,
        in_specs=(
            P(("dp", "group"), None),
            P(("dp", "group"), None),
            P(),
            P("dp", None, None),
            P("dp", "group", None),
            P("dp", "group"),
        ),
        out_specs=(P(("dp", "group"), None), P(("dp", "group"), None), P("group", None)),
        check_vma=False,
    )
```

```python
import functools
import math

import jax
import jax.numpy as jnp
from jax import lax
from jax.experimental import pallas as pl
from jax.experimental.pallas import tpu as pltpu
from jax.sharding import PartitionSpec as P

HD = 80
HEADS = 8
SLOT = 8
MASKED = -1e30
F32 = jnp.float32
BF16 = jnp.bfloat16
MESH = pl.DeviceIdType.MESH


TRACE = False
CUT = 2
RS_ORDER = (0, 3, 2, 1)
open_scope = []


def mark(name):
    if TRACE:
        if open_scope:
            open_scope.pop().__exit__(None, None, None)
        if name:
            scope = jax.named_scope(name)
            scope.__enter__()
            open_scope.append(scope)


def dot(a, b, dims=((1,), (0,))):
    return lax.dot_general(a, b, (dims, ((), ())), preferred_element_type=F32)


TN = ((0,), (0,))
NT = ((1,), (1,))


def iota(shape, dim):
    return lax.broadcasted_iota(jnp.int32, shape, dim)


def flat(x):
    g, s, c = x.shape
    return x.astype(F32).reshape(g * s, c).astype(BF16)


def partner(me, k):
    out, bit = me, 1
    while bit <= k:
        if k & bit:
            has = lax.rem(lax.div(me, bit), 2)
            out = out + bit * (1 - 2 * has)
        bit *= 2
    return out


def kernel(
    groups, reps,
    len_hbm, order_hbm, cut_hbm, qkv_hbm, cot_hbm, w_hbm,
    emb, grad, own,
    len_ref, order_ref, cut_ref, qkv, cot, w, sel, pack_t,
    sendq, recvq, sendg, recvg, cots, cotr, qbig, gbig, attall,
    grads, backs, backr, cot_t, spread, slot_rows, zsend, zbuf,
    in_sem,
    sq, rq, sg, rg, sc, rc, sa, ra, sb, rb, sz, rz, known,
):
    me = lax.axis_index("group")
    rep = lax.axis_index("dp")
    rows, feats3 = qkv.shape
    hf = feats3 // 3
    width = cot.shape[1]
    slots = groups * SLOT
    pack = slots // 2
    every = groups * pack
    share = width // groups
    folds = share // cots.shape[1]
    chunks = zbuf.shape[1]

    mark("m00_start")
    barrier = pltpu.get_barrier_semaphore()
    blocked = chunks % reps == 0
    order_k = list(range(groups - 1, 0, -1))
    for k in order_k:
        pl.semaphore_signal(
            barrier, inc=1, device_id={"group": partner(me, k)}, device_id_type=MESH
        )

    peers = (rep > 0).astype(jnp.int32) + (rep < reps - 1).astype(jnp.int32)

    def greet(sem):
        @pl.when(rep > 0)
        def _():
            pl.semaphore_signal(sem, inc=1, device_id={"dp": rep - 1}, device_id_type=MESH)

        @pl.when(rep < reps - 1)
        def _():
            pl.semaphore_signal(sem, inc=1, device_id={"dp": rep + 1}, device_id_type=MESH)

    greet(barrier)

    loads = [
        pltpu.make_async_copy(src, dst, in_sem.at[i])
        for i, (src, dst) in enumerate(
            (
                (qkv_hbm, qkv), (cot_hbm, cot), (w_hbm, w),
                (len_hbm, len_ref), (order_hbm, order_ref), (cut_hbm, cut_ref),
            )
        )
    ]
    for i in (3, 4, 0, 5):
        loads[i].start()

    mark("m01_book")
    for i in (3, 4):
        loads[i].wait()
    sub = iota((groups, groups), 0)
    lane = iota((groups, groups), 1)
    eye = sub == lane
    lens = len_ref[...].astype(F32)
    lens_row = len_ref[pl.ds(me, 1), :].astype(F32)
    turn_col = jnp.sum(
        jnp.where(order_ref[...] == sub, lane.astype(F32), 0.0), axis=1, keepdims=True
    )
    turn_row = jnp.sum(jnp.where(eye, turn_col, 0.0), axis=0, keepdims=True)
    len_col = jnp.sum(jnp.where(eye, lens_row, 0.0), axis=1, keepdims=True)
    start_col = jnp.sum(jnp.where(turn_row < turn_col, lens_row, 0.0), axis=1, keepdims=True)
    block_of = iota((slots, groups), 0) // SLOT == iota((slots, groups), 1)
    within = lax.rem(iota((slots, 1), 0), SLOT).astype(F32)

    def per_slot(column):
        wide = jnp.broadcast_to(column[:, :, None], (groups, SLOT, 1))
        return wide.reshape(slots, 1)

    send_start, send_len = per_slot(start_col), per_slot(len_col)
    send_pos = jnp.where(within < send_len, send_start + within, -1.0)
    sel[...] = jnp.where(send_pos == iota((slots, rows), 1).astype(F32), 1.0, 0.0).astype(BF16)

    def remote(src, dst, ssem, rsem, k):
        return pltpu.make_async_remote_copy(
            src_ref=src, dst_ref=dst, send_sem=ssem, recv_sem=rsem,
            device_id={"group": partner(me, k)}, device_id_type=MESH,
        )

    def exchange(src, dst, ssem, rsem):
        for k in order_k:
            remote(src.at[partner(me, k)], dst.at[me], ssem, rsem, k).start()
        pltpu.make_async_copy(src.at[me], dst.at[me], rsem).start()

    def arrived(dst, ssem, rsem):
        remote(dst, dst, ssem, rsem, 1).wait_recv()

    def departed(src, ssem, rsem):
        most = src.at[pl.ds(0, groups - 1)]
        remote(most, most, ssem, rsem, 1).wait_send()

    mark("m02_selq")
    loads[0].wait()
    loads[1].start()
    loads[2].start()
    sendq[...] = dot(sel[...], qkv[...]).reshape(groups, SLOT, feats3).astype(BF16)

    mark("m03_barrier")
    pl.semaphore_wait(barrier, groups - 1 + peers)
    if blocked:
        greet(known.at[0])

    mark("m04_sendq")
    exchange(sendq, recvq, sq.at[0], rq.at[0])

    mark("m05_attgrad")
    loads[1].wait()
    loads[2].wait()
    att_grad = dot(cot[...], w[...]).astype(BF16)
    sendg[...] = dot(sel[...], att_grad).reshape(groups, SLOT, hf).astype(BF16)
    mark("m06_cot")
    turned = dot(cot[...], sel[...], ((0,), (1,))).reshape(groups, folds, share // folds, slots)
    cots[...] = jnp.concatenate([turned[:, f] for f in range(folds)], axis=2).astype(BF16)

    mark("m065_book2")
    before = jnp.where(lane < sub, 1.0, 0.0).astype(BF16)
    lens_b = lens.astype(BF16)
    starts = dot(before, lens_b)
    expand = jnp.where(block_of, 1.0, 0.0).astype(BF16)
    starts_me = jnp.sum(jnp.where(lane == me, starts, 0.0), axis=1, keepdims=True).astype(BF16)
    lens_me = jnp.sum(jnp.where(lane == me, lens, 0.0), axis=1, keepdims=True).astype(BF16)
    pos_me = dot(expand, jnp.broadcast_to(starts_me, (groups, pack))) + within
    held_me = within < dot(expand, jnp.broadcast_to(lens_me, (groups, pack)))
    packs = iota((slots, pack), 1).astype(F32)
    pack_t[...] = jnp.where((pos_me == packs) & held_me, 1.0, 0.0).astype(BF16)

    fill = iota((groups, every), 1) // pack == iota((groups, every), 0)
    fill = jnp.where(fill, 1.0, 0.0).astype(BF16)
    first_of = dot(starts.astype(BF16), fill)
    count_of = dot(lens_b, fill)
    place_of = lax.rem(iota((groups, every), 1), pack).astype(F32) - first_of
    place_of = jnp.where((place_of >= 0.0) & (place_of < count_of), place_of, -1.0)
    slot_of = jnp.where(
        place_of >= 0.0, place_of + (iota((groups, every), 1) // pack * SLOT).astype(F32), -1.0
    )
    slot_row = iota((slots, every), 0).astype(F32)
    if folds > 1:
        for s in range(groups):
            spread[s * slots : (s + 1) * slots, :] = jnp.where(
                slot_row == slot_of[s : s + 1, :], 1.0, 0.0
            ).astype(BF16)
    else:
        slot_rows[...] = slot_of
    mine = jnp.sum(
        jnp.where(iota((groups, every), 0) == me, slot_of, 0.0), axis=0, keepdims=True
    )
    home = dot(
        sel[...], jnp.where(slot_row == mine, 1.0, 0.0).astype(BF16), TN
    ).astype(BF16)

    departed(sendq, sq.at[0], rq.at[0])
    exchange(cots, cotr, sc.at[0], rc.at[0])

    mark("m07_waitq")
    arrived(recvq, sq.at[0], rq.at[0])
    if blocked:
        for i in range(1, reps - 2):
            pl.semaphore_wait(known.at[i - 1], peers)
            greet(known.at[i])
    mark("m08_att")
    loads[5].wait()
    xq = dot(pack_t[...], flat(recvq[...]), TN).astype(BF16)
    query, keys, values = xq[:, :hf], xq[:, hf : 2 * hf], xq[:, 2 * hf :]
    feature = iota((1, hf), 1)
    heads = [
        (feature >= h * HD) & (feature < (h + 1) * HD) for h in range(HEADS)
    ]
    marks = [jnp.where(m, 1.0, 0.0).astype(BF16) for m in heads]
    for h in range(HEADS):
        qbig[h * pack : (h + 1) * pack, :] = query * marks[h]
    scale = 1.0 / math.sqrt(HD)
    cut = cut_ref[...]
    wide = HEADS * pack
    row_second = iota((pack, wide), 0) >= cut
    col_second = lax.rem(iota((pack, wide), 1), pack) >= cut
    same = row_second == col_second
    scores = dot(keys, qbig[...], NT) * scale
    scores = jnp.where(same, scores, MASKED)
    top = jnp.max(scores, axis=0, keepdims=True)
    expo = jnp.exp(scores - top)
    probs = expo / jnp.sum(expo, axis=0, keepdims=True)
    probs_b = probs.astype(BF16)

    def per_head(big):
        out = jnp.where(heads[0], big[:pack], 0.0)
        for h in range(1, HEADS):
            out = jnp.where(heads[h], big[h * pack : (h + 1) * pack], out)
        return out.astype(BF16)

    att = per_head(dot(probs_b, values, TN))
    attall[pl.ds(me, 1)] = att.reshape(1, pack, hf)
    direct = list(range(groups - 2, 0, -2))
    for k in direct:
        remote(attall.at[me], attall.at[me], sa.at[0], ra.at[k // 2], k).start()
    remote(attall.at[me], attall.at[me], sa.at[0], ra.at[0], 1).start()


    mark("m11_waitc")
    arrived(cotr, sc.at[0], rc.at[0])
    mark("m12_pack")
    if folds > 1:
        pieces = [cotr[s].astype(F32) for s in range(groups)]
        left = jnp.concatenate(
            [
                jnp.concatenate(
                    [piece[:, f * slots : (f + 1) * slots] for piece in pieces], axis=1
                )
                for f in range(folds)
            ],
            axis=0,
        ).astype(BF16)
        cot_t[...] = dot(left, spread[...]).astype(BF16)
    else:
        cot_t[...] = jnp.zeros(cot_t.shape, BF16)

        def place(s, carry):
            spread[...] = jnp.where(
                slot_row == slot_rows[pl.ds(s, 1), :], 1.0, 0.0
            ).astype(BF16)
            cot_t[...] = cot_t[...] + dot(cotr[s], spread[...]).astype(BF16)
            return carry

        lax.fori_loop(0, groups, place, 0)

    mark("m13_waita")
    for k in direct[::-1]:
        remote(attall.at[me], attall.at[me], sa.at[0], ra.at[k // 2], k).wait_recv()
        piece = attall.at[partner(me, k)]
        remote(piece, piece, sa.at[0], ra.at[0], 1).start()
    exchange(sendg, recvg, sg.at[0], rg.at[0])
    half = attall.at[pl.ds(0, groups // 2)]
    remote(half, half, sa.at[0], ra.at[0], 1).wait_recv()
    mark("m14_wg")
    att_rows = attall[...].reshape(every, hf)
    own[...] = dot(cot_t[...], att_rows).reshape(own.shape)

    def backward():
        mark("m09_waitg")
        arrived(recvg, sg.at[0], rg.at[0])
        mark("m10_bwd")
        xg = dot(pack_t[...], flat(recvg[...]), TN).astype(BF16)
        for h in range(HEADS):
            gbig[h * pack : (h + 1) * pack, :] = xg * marks[h]
        prob_grad = dot(values, gbig[...], NT)
        delta = jnp.sum(probs * prob_grad, axis=0, keepdims=True)
        score_grad = (probs * (prob_grad - delta) * scale).astype(BF16)
        grads[:, :hf] = per_head(dot(score_grad, keys, TN))
        grads[:, hf : 2 * hf] = dot(score_grad, qbig[...]).astype(BF16)
        grads[:, 2 * hf :] = dot(probs_b, gbig[...]).astype(BF16)

        backs[...] = dot(pack_t[...], grads[...]).reshape(groups, SLOT, feats3).astype(BF16)
        exchange(backs, backr, sb.at[0], rb.at[0])


    def project():
        mark("m16_emb")
        emb[...] = dot(dot(home, att_rows).astype(BF16), w[...], NT).astype(BF16)

    def source_rows():
        mark("m17_waitb")
        arrived(backr, sb.at[0], rb.at[0])
        mark("m18_back")
        grad[...] = dot(sel[...], flat(backr[...]), TN).astype(BF16)
        mark("m19_z")

    def along_line():
        mark("m15_zchain")
        @pl.when(rep == 0)
        def _():
            zbuf[0] = jnp.zeros(zbuf.shape[1:], BF16)

        @pl.when(rep == reps - 1)
        def _():
            zbuf[1] = jnp.zeros(zbuf.shape[1:], BF16)

        def hop(way, c):
            return pltpu.make_async_remote_copy(
                src_ref=zsend.at[way, c], dst_ref=zbuf.at[way, c],
                send_sem=sz.at[way], recv_sem=rz.at[way, c],
                device_id={"dp": rep + 1 - 2 * way}, device_id_type=MESH,
            )

        def step(way, c):
            spot = rep + way * (reps - 1 - 2 * rep)

            @pl.when(spot > 0)
            def _():
                hop(way, c).wait_recv()

            @pl.when(spot < reps - 1)
            def _():
                zsend[way, c] = (own[c] + zbuf[way, c].astype(F32)).astype(BF16)
                hop(way, c).start()

        near = (rep >= (reps + 1) // 2).astype(jnp.int32)
        edge = (rep == 0) | (rep == reps - 1)

        @pl.when(edge)
        def _():
            for c in range(chunks):
                step(near, c)

        backward()
        project()

        @pl.when(edge)
        def _():
            source_rows()
            for c in range(chunks):
                step(1 - near, c)

        @pl.when(jnp.logical_not(edge))
        def _():
            mark("m19_zmid")
            lag = chunks // 2
            for t in range(chunks + lag):
                if t < chunks:
                    step(near, t)
                if t >= lag:
                    step(1 - near, t - lag)
            source_rows()

        mark("m20_final")
        own[...] = own[...] + zbuf[0].astype(F32) + zbuf[1].astype(F32)

        for way in range(2):
            spot = rep + way * (reps - 1 - 2 * rep)

            @pl.when(spot < reps - 1)
            def _():
                pltpu.make_async_remote_copy(
                    src_ref=zsend.at[way], dst_ref=zbuf.at[way],
                    send_sem=sz.at[way], recv_sem=rz.at[way, 0],
                    device_id={"dp": rep + 1 - 2 * way}, device_id_type=MESH,
                ).wait_send()


    def by_blocks():
        size = chunks // reps
        cuts = [0, CUT, size] if size > CUT else [0, size]
        spans = list(zip(cuts[:-1], cuts[1:]))
        rounds = len(spans)

        def across(src, dst, i, to):
            return pltpu.make_async_remote_copy(
                src_ref=src, dst_ref=dst, send_sem=sz.at[i], recv_sem=rz.at[i, 0],
                device_id={"dp": to}, device_id_type=MESH,
            )

        mark("m15_scatter")
        pl.semaphore_wait(known.at[reps - 3], peers)
        zsend[0] = own[...].astype(BF16)
        for i, (low, high) in enumerate(spans):
            for to in RS_ORDER:

                @pl.when(rep != to)
                def _():
                    across(
                        zsend.at[0, pl.ds(to * size + low, high - low)],
                        zbuf.at[0, pl.ds(low * reps + rep * (high - low), high - low)],
                        i, to,
                    ).start()

        project()
        for i, (low, high) in enumerate(spans):
            wide = high - low
            mark(f"m17_waits{i}")
            most = zbuf.at[0, pl.ds(0, wide * (reps - 1))]
            across(most, most, i, rep).wait_recv()
            mark(f"m18_sum{i}")
            mine = pl.ds(rep * size + low, wide)
            zbuf[0, pl.ds(low * reps + rep * wide, wide)] = jnp.zeros(
                (wide,) + zbuf.shape[2:], BF16
            )
            total = own[mine]
            for r in range(reps):
                first = low * reps + r * wide
                total = total + zbuf[0, first : first + wide].astype(F32)
            zbuf[1, mine] = total.astype(BF16)
            for to in range(reps):

                @pl.when(rep != to)
                def _():
                    across(zbuf.at[1, mine], zbuf.at[1, mine], rounds + i, to).start()
            if i == 0:
                backward()

        source_rows()
        for i, (low, high) in enumerate(spans):
            most = zbuf.at[0, pl.ds(0, (high - low) * (reps - 1))]
            across(most, most, rounds + i, rep).wait_recv()
        mark("m20_final")
        own[...] = zbuf[1].astype(F32)
        for i in range(2 * rounds):
            low, high = spans[i % rounds]
            most = zbuf.at[0, pl.ds(0, (high - low) * (reps - 1))]
            across(most, most, i, rep).wait_send()

    if blocked:
        by_blocks()
    else:
        along_line()

    mark("m21_drain")
    departed(sendg, sg.at[0], rg.at[0])
    departed(cots, sc.at[0], rc.at[0])
    departed(backs, sb.at[0], rb.at[0])
    departed(attall, sa.at[0], ra.at[0])
    mark(None)


def write_out(emb, grad, own, emb_hbm, grad_hbm, wg_hbm, sems):
    pairs = ((emb, emb_hbm), (grad, grad_hbm), (own, wg_hbm))
    copies = [
        pltpu.make_async_copy(src, dst, sems.at[i]) for i, (src, dst) in enumerate(pairs)
    ]
    for copy in copies:
        copy.start()
    for copy in copies:
        copy.wait()


def local(groups, reps, qkv, embed_grad, out_weight, image_len, image_order, image_cut):
    rows, feats3 = qkv.shape
    width, hf = out_weight.shape
    slots = groups * SLOT
    pack = slots // 2
    share = width // groups
    part = 8 if share % (8 * reps) == 0 or share % 16 else 16
    chunks = share // part
    folds = 2 if slots < 128 and share % 32 == 0 else 1
    any_space = pl.BlockSpec(memory_space=pl.ANY)
    vmem = pl.BlockSpec(memory_space=pltpu.VMEM)
    dma = pltpu.SemaphoreType.DMA
    emb, grad, wg = pl.pallas_call(
        functools.partial(kernel, groups, reps),
        out_shape=(
            pltpu.VMEM((rows, width), BF16),
            pltpu.VMEM((rows, feats3), BF16),
            pltpu.VMEM((chunks, part, hf), F32),
        ),
        in_specs=[any_space] * 6,
        out_specs=(vmem, vmem, vmem),
        scratch_shapes=[
            pltpu.VMEM((groups, groups), jnp.int32),
            pltpu.VMEM((1, groups), jnp.int32),
            pltpu.VMEM((1, 1), jnp.int32),
            pltpu.VMEM((rows, feats3), BF16),
            pltpu.VMEM((rows, width), BF16),
            pltpu.VMEM((width, hf), BF16),
            pltpu.VMEM((slots, rows), BF16),
            pltpu.VMEM((slots, pack), BF16),
            pltpu.VMEM((groups, SLOT, feats3), BF16),
            pltpu.VMEM((groups, SLOT, feats3), BF16),
            pltpu.VMEM((groups, SLOT, hf), BF16),
            pltpu.VMEM((groups, SLOT, hf), BF16),
            pltpu.VMEM((groups, share // folds, slots * folds), BF16),
            pltpu.VMEM((groups, share // folds, slots * folds), BF16),
            pltpu.VMEM((HEADS * pack, hf), BF16),
            pltpu.VMEM((HEADS * pack, hf), BF16),
            pltpu.VMEM((groups, pack, hf), BF16),
            pltpu.VMEM((pack, feats3), BF16),
            pltpu.VMEM((groups, SLOT, feats3), BF16),
            pltpu.VMEM((groups, SLOT, feats3), BF16),
            pltpu.VMEM((share, groups * pack), BF16),
            pltpu.VMEM((groups * slots if folds > 1 else slots, groups * pack), BF16),
            pltpu.VMEM((groups, groups * pack), F32),
            pltpu.VMEM((2, chunks, part, hf), BF16),
            pltpu.VMEM((2, chunks, part, hf), BF16),
            dma((6,)),
        ]
        + [dma((1,)) for _ in range(6)]
        + [dma((1,)), dma((groups // 2,)), dma((1,)), dma((1,))]
        + ([dma((4,)), dma((4, 1))] if chunks % reps == 0 else [dma((2,)), dma((2, chunks))])
        + [pltpu.SemaphoreType.REGULAR((max(reps - 2, 1),))],
        compiler_params=pltpu.CompilerParams(
            collective_id=0, has_side_effects=True, vmem_limit_bytes=60 * 1024 * 1024
        ),
    )(
        image_len.reshape(groups, groups), image_order.reshape(1, groups), image_cut,
        qkv, embed_grad, out_weight,
    )
    emb, grad, wg = pl.pallas_call(
        write_out,
        out_shape=(
            jax.ShapeDtypeStruct((rows, width), BF16),
            jax.ShapeDtypeStruct((rows, feats3), BF16),
            jax.ShapeDtypeStruct((chunks, part, hf), F32),
        ),
        in_specs=[vmem, vmem, vmem],
        out_specs=(any_space, any_space, any_space),
        scratch_shapes=[dma((3,))],
    )(*(pltpu.with_memory_space_constraint(x, pltpu.VMEM) for x in (emb, grad, wg)))
    return emb, grad, wg.reshape(share, hf)


def solution(mesh):
    return jax.shard_map(
        functools.partial(local, mesh.shape["group"], mesh.shape["dp"]),
        mesh=mesh,
        in_specs=(
            P(("dp", "group"), None),
            P(("dp", "group"), None),
            P(),
            P("dp", None, None),
            P("dp", "group", None),
            P("dp", "group"),
        ),
        out_specs=(P(("dp", "group"), None), P(("dp", "group"), None), P("group", None)),
        check_vma=False,
    )
```

```python
import functools
import math

import jax
import jax.numpy as jnp
from jax import lax
from jax.experimental import pallas as pl
from jax.experimental.pallas import tpu as pltpu
from jax.sharding import PartitionSpec as P

HD = 80
HEADS = 8
SLOT = 8
MASKED = -1e30
F32 = jnp.float32
BF16 = jnp.bfloat16
MESH = pl.DeviceIdType.MESH


TRACE = False
CUT = 2
RS_ORDER = (3, 0, 1, 2)
open_scope = []


def mark(name):
    if TRACE:
        if open_scope:
            open_scope.pop().__exit__(None, None, None)
        if name:
            scope = jax.named_scope(name)
            scope.__enter__()
            open_scope.append(scope)


def dot(a, b, dims=((1,), (0,))):
    return lax.dot_general(a, b, (dims, ((), ())), preferred_element_type=F32)


TN = ((0,), (0,))
NT = ((1,), (1,))


def iota(shape, dim):
    return lax.broadcasted_iota(jnp.int32, shape, dim)


def flat(x):
    g, s, c = x.shape
    return x.astype(F32).reshape(g * s, c).astype(BF16)


def partner(me, k):
    out, bit = me, 1
    while bit <= k:
        if k & bit:
            has = lax.rem(lax.div(me, bit), 2)
            out = out + bit * (1 - 2 * has)
        bit *= 2
    return out


def kernel(
    groups, reps,
    len_hbm, order_hbm, cut_hbm, qkv_hbm, cot_hbm, w_hbm,
    emb, grad, own,
    len_ref, order_ref, cut_ref, qkv, cot, w, sel, pack_t,
    sendq, recvq, sendg, recvg, cots, cotr, qbig, gbig, attall,
    grads, backs, backr, cot_t, spread, slot_rows, zsend, zbuf,
    in_sem,
    sq, rq, sg, rg, sc, rc, sa, ra, sb, rb, sz, rz, known,
):
    me = lax.axis_index("group")
    rep = lax.axis_index("dp")
    rows, feats3 = qkv.shape
    hf = feats3 // 3
    width = cot.shape[1]
    slots = groups * SLOT
    pack = slots // 2
    every = groups * pack
    share = width // groups
    folds = share // cots.shape[1]
    chunks = zbuf.shape[1]

    mark("m00_start")
    barrier = pltpu.get_barrier_semaphore()
    blocked = chunks % reps == 0
    order_k = list(range(groups - 1, 0, -1))
    for k in order_k:
        pl.semaphore_signal(
            barrier, inc=1, device_id={"group": partner(me, k)}, device_id_type=MESH
        )

    peers = (rep > 0).astype(jnp.int32) + (rep < reps - 1).astype(jnp.int32)

    def greet(sem):
        @pl.when(rep > 0)
        def _():
            pl.semaphore_signal(sem, inc=1, device_id={"dp": rep - 1}, device_id_type=MESH)

        @pl.when(rep < reps - 1)
        def _():
            pl.semaphore_signal(sem, inc=1, device_id={"dp": rep + 1}, device_id_type=MESH)

    greet(barrier)

    loads = [
        pltpu.make_async_copy(src, dst, in_sem.at[i])
        for i, (src, dst) in enumerate(
            (
                (qkv_hbm, qkv), (cot_hbm, cot), (w_hbm, w),
                (len_hbm, len_ref), (order_hbm, order_ref), (cut_hbm, cut_ref),
            )
        )
    ]
    for i in (3, 4, 0, 5):
        loads[i].start()

    mark("m01_book")
    for i in (3, 4):
        loads[i].wait()
    sub = iota((groups, groups), 0)
    lane = iota((groups, groups), 1)
    eye = sub == lane
    lens = len_ref[...].astype(F32)
    lens_row = len_ref[pl.ds(me, 1), :].astype(F32)
    turn_col = jnp.sum(
        jnp.where(order_ref[...] == sub, lane.astype(F32), 0.0), axis=1, keepdims=True
    )
    turn_row = jnp.sum(jnp.where(eye, turn_col, 0.0), axis=0, keepdims=True)
    len_col = jnp.sum(jnp.where(eye, lens_row, 0.0), axis=1, keepdims=True)
    start_col = jnp.sum(jnp.where(turn_row < turn_col, lens_row, 0.0), axis=1, keepdims=True)
    block_of = iota((slots, groups), 0) // SLOT == iota((slots, groups), 1)
    within = lax.rem(iota((slots, 1), 0), SLOT).astype(F32)

    def per_slot(column):
        wide = jnp.broadcast_to(column[:, :, None], (groups, SLOT, 1))
        return wide.reshape(slots, 1)

    send_start, send_len = per_slot(start_col), per_slot(len_col)
    send_pos = jnp.where(within < send_len, send_start + within, -1.0)
    sel[...] = jnp.where(send_pos == iota((slots, rows), 1).astype(F32), 1.0, 0.0).astype(BF16)

    def remote(src, dst, ssem, rsem, k):
        return pltpu.make_async_remote_copy(
            src_ref=src, dst_ref=dst, send_sem=ssem, recv_sem=rsem,
            device_id={"group": partner(me, k)}, device_id_type=MESH,
        )

    def exchange(src, dst, ssem, rsem):
        for k in order_k:
            remote(src.at[partner(me, k)], dst.at[me], ssem, rsem, k).start()
        pltpu.make_async_copy(src.at[me], dst.at[me], rsem).start()

    def arrived(dst, ssem, rsem):
        remote(dst, dst, ssem, rsem, 1).wait_recv()

    def departed(src, ssem, rsem):
        most = src.at[pl.ds(0, groups - 1)]
        remote(most, most, ssem, rsem, 1).wait_send()

    mark("m02_selq")
    loads[0].wait()
    loads[1].start()
    loads[2].start()
    sendq[...] = dot(sel[...], qkv[...]).reshape(groups, SLOT, feats3).astype(BF16)

    mark("m03_barrier")
    pl.semaphore_wait(barrier, groups - 1 + peers)
    if blocked:
        greet(known.at[0])

    mark("m04_sendq")
    exchange(sendq, recvq, sq.at[0], rq.at[0])

    mark("m05_attgrad")
    loads[1].wait()
    loads[2].wait()
    att_grad = dot(cot[...], w[...]).astype(BF16)
    sendg[...] = dot(sel[...], att_grad).reshape(groups, SLOT, hf).astype(BF16)
    mark("m06_cot")
    turned = dot(cot[...], sel[...], ((0,), (1,))).reshape(groups, folds, share // folds, slots)
    cots[...] = jnp.concatenate([turned[:, f] for f in range(folds)], axis=2).astype(BF16)

    mark("m065_book2")
    before = jnp.where(lane < sub, 1.0, 0.0).astype(BF16)
    lens_b = lens.astype(BF16)
    starts = dot(before, lens_b)
    expand = jnp.where(block_of, 1.0, 0.0).astype(BF16)
    starts_me = jnp.sum(jnp.where(lane == me, starts, 0.0), axis=1, keepdims=True).astype(BF16)
    lens_me = jnp.sum(jnp.where(lane == me, lens, 0.0), axis=1, keepdims=True).astype(BF16)
    pos_me = dot(expand, jnp.broadcast_to(starts_me, (groups, pack))) + within
    held_me = within < dot(expand, jnp.broadcast_to(lens_me, (groups, pack)))
    packs = iota((slots, pack), 1).astype(F32)
    pack_t[...] = jnp.where((pos_me == packs) & held_me, 1.0, 0.0).astype(BF16)

    fill = iota((groups, every), 1) // pack == iota((groups, every), 0)
    fill = jnp.where(fill, 1.0, 0.0).astype(BF16)
    first_of = dot(starts.astype(BF16), fill)
    count_of = dot(lens_b, fill)
    place_of = lax.rem(iota((groups, every), 1), pack).astype(F32) - first_of
    place_of = jnp.where((place_of >= 0.0) & (place_of < count_of), place_of, -1.0)
    slot_of = jnp.where(
        place_of >= 0.0, place_of + (iota((groups, every), 1) // pack * SLOT).astype(F32), -1.0
    )
    slot_row = iota((slots, every), 0).astype(F32)
    if folds > 1:
        for s in range(groups):
            spread[s * slots : (s + 1) * slots, :] = jnp.where(
                slot_row == slot_of[s : s + 1, :], 1.0, 0.0
            ).astype(BF16)
    else:
        slot_rows[...] = slot_of
    mine = jnp.sum(
        jnp.where(iota((groups, every), 0) == me, slot_of, 0.0), axis=0, keepdims=True
    )
    home = dot(
        sel[...], jnp.where(slot_row == mine, 1.0, 0.0).astype(BF16), TN
    ).astype(BF16)

    departed(sendq, sq.at[0], rq.at[0])
    exchange(cots, cotr, sc.at[0], rc.at[0])

    mark("m07_waitq")
    arrived(recvq, sq.at[0], rq.at[0])
    if blocked:
        for i in range(1, reps - 2):
            pl.semaphore_wait(known.at[i - 1], peers)
            greet(known.at[i])
    mark("m08_att")
    loads[5].wait()
    xq = dot(pack_t[...], flat(recvq[...]), TN).astype(BF16)
    query, keys, values = xq[:, :hf], xq[:, hf : 2 * hf], xq[:, 2 * hf :]
    feature = iota((1, hf), 1)
    heads = [
        (feature >= h * HD) & (feature < (h + 1) * HD) for h in range(HEADS)
    ]
    marks = [jnp.where(m, 1.0, 0.0).astype(BF16) for m in heads]
    for h in range(HEADS):
        qbig[h * pack : (h + 1) * pack, :] = query * marks[h]
    scale = 1.0 / math.sqrt(HD)
    cut = cut_ref[...]
    wide = HEADS * pack
    row_second = iota((pack, wide), 0) >= cut
    col_second = lax.rem(iota((pack, wide), 1), pack) >= cut
    same = row_second == col_second
    scores = dot(keys, qbig[...], NT) * scale
    scores = jnp.where(same, scores, MASKED)
    top = jnp.max(scores, axis=0, keepdims=True)
    expo = jnp.exp(scores - top)
    probs = expo / jnp.sum(expo, axis=0, keepdims=True)
    probs_b = probs.astype(BF16)

    def per_head(big):
        out = jnp.where(heads[0], big[:pack], 0.0)
        for h in range(1, HEADS):
            out = jnp.where(heads[h], big[h * pack : (h + 1) * pack], out)
        return out.astype(BF16)

    att = per_head(dot(probs_b, values, TN))
    attall[pl.ds(me, 1)] = att.reshape(1, pack, hf)
    direct = list(range(groups - 2, 0, -2))
    remote(attall.at[me], attall.at[me], sa.at[0], ra.at[0], 1).start()
    for k in direct:
        remote(attall.at[me], attall.at[me], sa.at[0], ra.at[k // 2], k).start()


    mark("m11_waitc")
    arrived(cotr, sc.at[0], rc.at[0])
    mark("m12_pack")
    if folds > 1:
        pieces = [cotr[s].astype(F32) for s in range(groups)]
        left = jnp.concatenate(
            [
                jnp.concatenate(
                    [piece[:, f * slots : (f + 1) * slots] for piece in pieces], axis=1
                )
                for f in range(folds)
            ],
            axis=0,
        ).astype(BF16)
        cot_t[...] = dot(left, spread[...]).astype(BF16)
    else:
        cot_t[...] = jnp.zeros(cot_t.shape, BF16)

        def place(s, carry):
            spread[...] = jnp.where(
                slot_row == slot_rows[pl.ds(s, 1), :], 1.0, 0.0
            ).astype(BF16)
            cot_t[...] = cot_t[...] + dot(cotr[s], spread[...]).astype(BF16)
            return carry

        lax.fori_loop(0, groups, place, 0)

    mark("m13_waita")
    for k in direct[::-1]:
        remote(attall.at[me], attall.at[me], sa.at[0], ra.at[k // 2], k).wait_recv()
        piece = attall.at[partner(me, k)]
        remote(piece, piece, sa.at[0], ra.at[0], 1).start()
    exchange(sendg, recvg, sg.at[0], rg.at[0])
    half = attall.at[pl.ds(0, groups // 2)]
    remote(half, half, sa.at[0], ra.at[0], 1).wait_recv()
    mark("m14_wg")
    att_rows = attall[...].reshape(every, hf)
    own[...] = dot(cot_t[...], att_rows).reshape(own.shape)

    def backward():
        mark("m09_waitg")
        arrived(recvg, sg.at[0], rg.at[0])
        mark("m10_bwd")
        xg = dot(pack_t[...], flat(recvg[...]), TN).astype(BF16)
        for h in range(HEADS):
            gbig[h * pack : (h + 1) * pack, :] = xg * marks[h]
        prob_grad = dot(values, gbig[...], NT)
        delta = jnp.sum(probs * prob_grad, axis=0, keepdims=True)
        score_grad = (probs * (prob_grad - delta) * scale).astype(BF16)
        grads[:, :hf] = per_head(dot(score_grad, keys, TN))
        grads[:, hf : 2 * hf] = dot(score_grad, qbig[...]).astype(BF16)
        grads[:, 2 * hf :] = dot(probs_b, gbig[...]).astype(BF16)

        backs[...] = dot(pack_t[...], grads[...]).reshape(groups, SLOT, feats3).astype(BF16)
        exchange(backs, backr, sb.at[0], rb.at[0])


    def project():
        mark("m16_emb")
        emb[...] = dot(dot(home, att_rows).astype(BF16), w[...], NT).astype(BF16)

    def source_rows():
        mark("m17_waitb")
        arrived(backr, sb.at[0], rb.at[0])
        mark("m18_back")
        grad[...] = dot(sel[...], flat(backr[...]), TN).astype(BF16)
        mark("m19_z")

    def along_line():
        mark("m15_zchain")
        @pl.when(rep == 0)
        def _():
            zbuf[0] = jnp.zeros(zbuf.shape[1:], BF16)

        @pl.when(rep == reps - 1)
        def _():
            zbuf[1] = jnp.zeros(zbuf.shape[1:], BF16)

        def hop(way, c):
            return pltpu.make_async_remote_copy(
                src_ref=zsend.at[way, c], dst_ref=zbuf.at[way, c],
                send_sem=sz.at[way], recv_sem=rz.at[way, c],
                device_id={"dp": rep + 1 - 2 * way}, device_id_type=MESH,
            )

        def step(way, c):
            spot = rep + way * (reps - 1 - 2 * rep)

            @pl.when(spot > 0)
            def _():
                hop(way, c).wait_recv()

            @pl.when(spot < reps - 1)
            def _():
                zsend[way, c] = (own[c] + zbuf[way, c].astype(F32)).astype(BF16)
                hop(way, c).start()

        near = (rep >= (reps + 1) // 2).astype(jnp.int32)
        edge = (rep == 0) | (rep == reps - 1)

        @pl.when(edge)
        def _():
            for c in range(chunks):
                step(near, c)

        backward()
        project()

        @pl.when(edge)
        def _():
            source_rows()
            for c in range(chunks):
                step(1 - near, c)

        @pl.when(jnp.logical_not(edge))
        def _():
            mark("m19_zmid")
            lag = chunks // 2
            for t in range(chunks + lag):
                if t < chunks:
                    step(near, t)
                if t >= lag:
                    step(1 - near, t - lag)
            source_rows()

        mark("m20_final")
        own[...] = own[...] + zbuf[0].astype(F32) + zbuf[1].astype(F32)

        for way in range(2):
            spot = rep + way * (reps - 1 - 2 * rep)

            @pl.when(spot < reps - 1)
            def _():
                pltpu.make_async_remote_copy(
                    src_ref=zsend.at[way], dst_ref=zbuf.at[way],
                    send_sem=sz.at[way], recv_sem=rz.at[way, 0],
                    device_id={"dp": rep + 1 - 2 * way}, device_id_type=MESH,
                ).wait_send()


    def by_blocks():
        size = chunks // reps
        cuts = [0, CUT, size] if size > CUT else [0, size]
        spans = list(zip(cuts[:-1], cuts[1:]))
        rounds = len(spans)

        def across(src, dst, i, to):
            return pltpu.make_async_remote_copy(
                src_ref=src, dst_ref=dst, send_sem=sz.at[i], recv_sem=rz.at[i, 0],
                device_id={"dp": to}, device_id_type=MESH,
            )

        mark("m15_scatter")
        pl.semaphore_wait(known.at[reps - 3], peers)
        zsend[0] = own[...].astype(BF16)
        for i, (low, high) in enumerate(spans):
            for to in RS_ORDER:

                @pl.when(rep != to)
                def _():
                    across(
                        zsend.at[0, pl.ds(to * size + low, high - low)],
                        zbuf.at[0, pl.ds(low * reps + rep * (high - low), high - low)],
                        i, to,
                    ).start()

        project()
        for i, (low, high) in enumerate(spans):
            wide = high - low
            mark(f"m17_waits{i}")
            most = zbuf.at[0, pl.ds(0, wide * (reps - 1))]
            across(most, most, i, rep).wait_recv()
            mark(f"m18_sum{i}")
            mine = pl.ds(rep * size + low, wide)
            zbuf[0, pl.ds(low * reps + rep * wide, wide)] = jnp.zeros(
                (wide,) + zbuf.shape[2:], BF16
            )
            total = own[mine]
            for r in range(reps):
                first = low * reps + r * wide
                total = total + zbuf[0, first : first + wide].astype(F32)
            zbuf[1, mine] = total.astype(BF16)
            for to in range(reps):

                @pl.when(rep != to)
                def _():
                    across(zbuf.at[1, mine], zbuf.at[1, mine], rounds + i, to).start()
            if i == 0:
                backward()

        source_rows()
        for i, (low, high) in enumerate(spans):
            most = zbuf.at[0, pl.ds(0, (high - low) * (reps - 1))]
            across(most, most, rounds + i, rep).wait_recv()
        mark("m20_final")
        own[...] = zbuf[1].astype(F32)
        for i in range(2 * rounds):
            low, high = spans[i % rounds]
            most = zbuf.at[0, pl.ds(0, (high - low) * (reps - 1))]
            across(most, most, i, rep).wait_send()

    if blocked:
        by_blocks()
    else:
        along_line()

    mark("m21_drain")
    departed(sendg, sg.at[0], rg.at[0])
    departed(cots, sc.at[0], rc.at[0])
    departed(backs, sb.at[0], rb.at[0])
    departed(attall, sa.at[0], ra.at[0])
    mark(None)


def write_out(emb, grad, own, emb_hbm, grad_hbm, wg_hbm, sems):
    pairs = ((emb, emb_hbm), (grad, grad_hbm), (own, wg_hbm))
    copies = [
        pltpu.make_async_copy(src, dst, sems.at[i]) for i, (src, dst) in enumerate(pairs)
    ]
    for copy in copies:
        copy.start()
    for copy in copies:
        copy.wait()


def local(groups, reps, qkv, embed_grad, out_weight, image_len, image_order, image_cut):
    rows, feats3 = qkv.shape
    width, hf = out_weight.shape
    slots = groups * SLOT
    pack = slots // 2
    share = width // groups
    part = 8 if share % (8 * reps) == 0 or share % 16 else 16
    chunks = share // part
    folds = 2 if slots < 128 and share % 32 == 0 else 1
    any_space = pl.BlockSpec(memory_space=pl.ANY)
    vmem = pl.BlockSpec(memory_space=pltpu.VMEM)
    dma = pltpu.SemaphoreType.DMA
    emb, grad, wg = pl.pallas_call(
        functools.partial(kernel, groups, reps),
        out_shape=(
            pltpu.VMEM((rows, width), BF16),
            pltpu.VMEM((rows, feats3), BF16),
            pltpu.VMEM((chunks, part, hf), F32),
        ),
        in_specs=[any_space] * 6,
        out_specs=(vmem, vmem, vmem),
        scratch_shapes=[
            pltpu.VMEM((groups, groups), jnp.int32),
            pltpu.VMEM((1, groups), jnp.int32),
            pltpu.VMEM((1, 1), jnp.int32),
            pltpu.VMEM((rows, feats3), BF16),
            pltpu.VMEM((rows, width), BF16),
            pltpu.VMEM((width, hf), BF16),
            pltpu.VMEM((slots, rows), BF16),
            pltpu.VMEM((slots, pack), BF16),
            pltpu.VMEM((groups, SLOT, feats3), BF16),
            pltpu.VMEM((groups, SLOT, feats3), BF16),
            pltpu.VMEM((groups, SLOT, hf), BF16),
            pltpu.VMEM((groups, SLOT, hf), BF16),
            pltpu.VMEM((groups, share // folds, slots * folds), BF16),
            pltpu.VMEM((groups, share // folds, slots * folds), BF16),
            pltpu.VMEM((HEADS * pack, hf), BF16),
            pltpu.VMEM((HEADS * pack, hf), BF16),
            pltpu.VMEM((groups, pack, hf), BF16),
            pltpu.VMEM((pack, feats3), BF16),
            pltpu.VMEM((groups, SLOT, feats3), BF16),
            pltpu.VMEM((groups, SLOT, feats3), BF16),
            pltpu.VMEM((share, groups * pack), BF16),
            pltpu.VMEM((groups * slots if folds > 1 else slots, groups * pack), BF16),
            pltpu.VMEM((groups, groups * pack), F32),
            pltpu.VMEM((2, chunks, part, hf), BF16),
            pltpu.VMEM((2, chunks, part, hf), BF16),
            dma((6,)),
        ]
        + [dma((1,)) for _ in range(6)]
        + [dma((1,)), dma((groups // 2,)), dma((1,)), dma((1,))]
        + ([dma((4,)), dma((4, 1))] if chunks % reps == 0 else [dma((2,)), dma((2, chunks))])
        + [pltpu.SemaphoreType.REGULAR((max(reps - 2, 1),))],
        compiler_params=pltpu.CompilerParams(
            collective_id=0, has_side_effects=True, vmem_limit_bytes=60 * 1024 * 1024
        ),
    )(
        image_len.reshape(groups, groups), image_order.reshape(1, groups), image_cut,
        qkv, embed_grad, out_weight,
    )
    emb, grad, wg = pl.pallas_call(
        write_out,
        out_shape=(
            jax.ShapeDtypeStruct((rows, width), BF16),
            jax.ShapeDtypeStruct((rows, feats3), BF16),
            jax.ShapeDtypeStruct((chunks, part, hf), F32),
        ),
        in_specs=[vmem, vmem, vmem],
        out_specs=(any_space, any_space, any_space),
        scratch_shapes=[dma((3,))],
    )(*(pltpu.with_memory_space_constraint(x, pltpu.VMEM) for x in (emb, grad, wg)))
    return emb, grad, wg.reshape(share, hf)


def solution(mesh):
    return jax.shard_map(
        functools.partial(local, mesh.shape["group"], mesh.shape["dp"]),
        mesh=mesh,
        in_specs=(
            P(("dp", "group"), None),
            P(("dp", "group"), None),
            P(),
            P("dp", None, None),
            P("dp", "group", None),
            P("dp", "group"),
        ),
        out_specs=(P(("dp", "group"), None), P(("dp", "group"), None), P("group", None)),
        check_vma=False,
    )
```

```python
import functools
import math

import jax
import jax.numpy as jnp
from jax import lax
from jax.experimental import pallas as pl
from jax.experimental.pallas import tpu as pltpu
from jax.sharding import PartitionSpec as P

HD = 80
HEADS = 8
SLOT = 8
MASKED = -1e30
F32 = jnp.float32
BF16 = jnp.bfloat16
MESH = pl.DeviceIdType.MESH


TRACE = False
CUT = 2
open_scope = []


def mark(name):
    if TRACE:
        if open_scope:
            open_scope.pop().__exit__(None, None, None)
        if name:
            scope = jax.named_scope(name)
            scope.__enter__()
            open_scope.append(scope)


def dot(a, b, dims=((1,), (0,))):
    return lax.dot_general(a, b, (dims, ((), ())), preferred_element_type=F32)


TN = ((0,), (0,))
NT = ((1,), (1,))


def iota(shape, dim):
    return lax.broadcasted_iota(jnp.int32, shape, dim)


def flat(x):
    g, s, c = x.shape
    return x.astype(F32).reshape(g * s, c).astype(BF16)


def partner(me, k):
    out, bit = me, 1
    while bit <= k:
        if k & bit:
            has = lax.rem(lax.div(me, bit), 2)
            out = out + bit * (1 - 2 * has)
        bit *= 2
    return out


def kernel(
    groups, reps,
    len_hbm, order_hbm, cut_hbm, qkv_hbm, cot_hbm, w_hbm,
    emb, grad, own,
    len_ref, order_ref, cut_ref, qkv, cot, w, sel, pack_t,
    sendq, recvq, sendg, recvg, cots, cotr, qbig, gbig, attall,
    grads, backs, backr, cot_t, spread, slot_rows, zsend, zbuf,
    in_sem,
    sq, rq, sg, rg, sc, rc, sa, ra, sb, rb, sz, rz, known,
):
    me = lax.axis_index("group")
    rep = lax.axis_index("dp")
    rows, feats3 = qkv.shape
    hf = feats3 // 3
    width = cot.shape[1]
    slots = groups * SLOT
    pack = slots // 2
    every = groups * pack
    share = width // groups
    folds = share // cots.shape[1]
    chunks = zbuf.shape[1]

    mark("m00_start")
    barrier = pltpu.get_barrier_semaphore()
    blocked = chunks % reps == 0
    order_k = list(range(groups - 1, 0, -1))
    for k in order_k:
        pl.semaphore_signal(
            barrier, inc=1, device_id={"group": partner(me, k)}, device_id_type=MESH
        )

    peers = (rep > 0).astype(jnp.int32) + (rep < reps - 1).astype(jnp.int32)

    def greet(sem):
        @pl.when(rep > 0)
        def _():
            pl.semaphore_signal(sem, inc=1, device_id={"dp": rep - 1}, device_id_type=MESH)

        @pl.when(rep < reps - 1)
        def _():
            pl.semaphore_signal(sem, inc=1, device_id={"dp": rep + 1}, device_id_type=MESH)

    greet(barrier)

    loads = [
        pltpu.make_async_copy(src, dst, in_sem.at[i])
        for i, (src, dst) in enumerate(
            (
                (qkv_hbm, qkv), (cot_hbm, cot), (w_hbm, w),
                (len_hbm, len_ref), (order_hbm, order_ref), (cut_hbm, cut_ref),
            )
        )
    ]
    for i in (3, 4, 0, 5):
        loads[i].start()

    mark("m01_book")
    for i in (3, 4):
        loads[i].wait()
    sub = iota((groups, groups), 0)
    lane = iota((groups, groups), 1)
    eye = sub == lane
    lens = len_ref[...].astype(F32)
    lens_row = len_ref[pl.ds(me, 1), :].astype(F32)
    turn_col = jnp.sum(
        jnp.where(order_ref[...] == sub, lane.astype(F32), 0.0), axis=1, keepdims=True
    )
    turn_row = jnp.sum(jnp.where(eye, turn_col, 0.0), axis=0, keepdims=True)
    len_col = jnp.sum(jnp.where(eye, lens_row, 0.0), axis=1, keepdims=True)
    start_col = jnp.sum(jnp.where(turn_row < turn_col, lens_row, 0.0), axis=1, keepdims=True)
    block_of = iota((slots, groups), 0) // SLOT == iota((slots, groups), 1)
    within = lax.rem(iota((slots, 1), 0), SLOT).astype(F32)

    def per_slot(column):
        wide = jnp.broadcast_to(column[:, :, None], (groups, SLOT, 1))
        return wide.reshape(slots, 1)

    send_start, send_len = per_slot(start_col), per_slot(len_col)
    send_pos = jnp.where(within < send_len, send_start + within, -1.0)
    sel[...] = jnp.where(send_pos == iota((slots, rows), 1).astype(F32), 1.0, 0.0).astype(BF16)

    def remote(src, dst, ssem, rsem, k):
        return pltpu.make_async_remote_copy(
            src_ref=src, dst_ref=dst, send_sem=ssem, recv_sem=rsem,
            device_id={"group": partner(me, k)}, device_id_type=MESH,
        )

    def exchange(src, dst, ssem, rsem):
        for k in order_k:
            remote(src.at[partner(me, k)], dst.at[me], ssem, rsem, k).start()
        pltpu.make_async_copy(src.at[me], dst.at[me], rsem).start()

    def arrived(dst, ssem, rsem):
        remote(dst, dst, ssem, rsem, 1).wait_recv()

    def departed(src, ssem, rsem):
        most = src.at[pl.ds(0, groups - 1)]
        remote(most, most, ssem, rsem, 1).wait_send()

    mark("m02_selq")
    loads[0].wait()
    loads[1].start()
    loads[2].start()
    sendq[...] = dot(sel[...], qkv[...]).reshape(groups, SLOT, feats3).astype(BF16)

    mark("m03_barrier")
    pl.semaphore_wait(barrier, groups - 1 + peers)
    if blocked:
        greet(known.at[0])

    mark("m04_sendq")
    exchange(sendq, recvq, sq.at[0], rq.at[0])

    mark("m05_attgrad")
    loads[1].wait()
    loads[2].wait()
    att_grad = dot(cot[...], w[...]).astype(BF16)
    sendg[...] = dot(sel[...], att_grad).reshape(groups, SLOT, hf).astype(BF16)
    mark("m06_cot")
    turned = dot(cot[...], sel[...], ((0,), (1,))).reshape(groups, folds, share // folds, slots)
    cots[...] = jnp.concatenate([turned[:, f] for f in range(folds)], axis=2).astype(BF16)

    mark("m065_book2")
    before = jnp.where(lane < sub, 1.0, 0.0).astype(BF16)
    lens_b = lens.astype(BF16)
    starts = dot(before, lens_b)
    expand = jnp.where(block_of, 1.0, 0.0).astype(BF16)
    starts_me = jnp.sum(jnp.where(lane == me, starts, 0.0), axis=1, keepdims=True).astype(BF16)
    lens_me = jnp.sum(jnp.where(lane == me, lens, 0.0), axis=1, keepdims=True).astype(BF16)
    pos_me = dot(expand, jnp.broadcast_to(starts_me, (groups, pack))) + within
    held_me = within < dot(expand, jnp.broadcast_to(lens_me, (groups, pack)))
    packs = iota((slots, pack), 1).astype(F32)
    pack_t[...] = jnp.where((pos_me == packs) & held_me, 1.0, 0.0).astype(BF16)

    fill = iota((groups, every), 1) // pack == iota((groups, every), 0)
    fill = jnp.where(fill, 1.0, 0.0).astype(BF16)
    first_of = dot(starts.astype(BF16), fill)
    count_of = dot(lens_b, fill)
    place_of = lax.rem(iota((groups, every), 1), pack).astype(F32) - first_of
    place_of = jnp.where((place_of >= 0.0) & (place_of < count_of), place_of, -1.0)
    slot_of = jnp.where(
        place_of >= 0.0, place_of + (iota((groups, every), 1) // pack * SLOT).astype(F32), -1.0
    )
    slot_row = iota((slots, every), 0).astype(F32)
    if folds > 1:
        for s in range(groups):
            spread[s * slots : (s + 1) * slots, :] = jnp.where(
                slot_row == slot_of[s : s + 1, :], 1.0, 0.0
            ).astype(BF16)
    else:
        slot_rows[...] = slot_of
    mine = jnp.sum(
        jnp.where(iota((groups, every), 0) == me, slot_of, 0.0), axis=0, keepdims=True
    )
    home = dot(
        sel[...], jnp.where(slot_row == mine, 1.0, 0.0).astype(BF16), TN
    ).astype(BF16)

    departed(sendq, sq.at[0], rq.at[0])
    exchange(cots, cotr, sc.at[0], rc.at[0])

    mark("m07_waitq")
    arrived(recvq, sq.at[0], rq.at[0])
    if blocked:
        for i in range(1, reps - 2):
            pl.semaphore_wait(known.at[i - 1], peers)
            greet(known.at[i])
    mark("m08_att")
    loads[5].wait()
    xq = dot(pack_t[...], flat(recvq[...]), TN).astype(BF16)
    query, keys, values = xq[:, :hf], xq[:, hf : 2 * hf], xq[:, 2 * hf :]
    feature = iota((1, hf), 1)
    heads = [
        (feature >= h * HD) & (feature < (h + 1) * HD) for h in range(HEADS)
    ]
    marks = [jnp.where(m, 1.0, 0.0).astype(BF16) for m in heads]
    for h in range(HEADS):
        qbig[h * pack : (h + 1) * pack, :] = query * marks[h]
    scale = 1.0 / math.sqrt(HD)
    cut = cut_ref[...]
    wide = HEADS * pack
    row_second = iota((pack, wide), 0) >= cut
    col_second = lax.rem(iota((pack, wide), 1), pack) >= cut
    same = row_second == col_second
    scores = dot(keys, qbig[...], NT) * scale
    scores = jnp.where(same, scores, MASKED)
    top = jnp.max(scores, axis=0, keepdims=True)
    expo = jnp.exp(scores - top)
    probs = expo / jnp.sum(expo, axis=0, keepdims=True)
    probs_b = probs.astype(BF16)

    def per_head(big):
        out = jnp.where(heads[0], big[:pack], 0.0)
        for h in range(1, HEADS):
            out = jnp.where(heads[h], big[h * pack : (h + 1) * pack], out)
        return out.astype(BF16)

    att = per_head(dot(probs_b, values, TN))
    attall[pl.ds(me, 1)] = att.reshape(1, pack, hf)
    direct = list(range(groups - 2, 0, -2))
    remote(attall.at[me], attall.at[me], sa.at[0], ra.at[0], 1).start()
    for k in direct:
        remote(attall.at[me], attall.at[me], sa.at[0], ra.at[k // 2], k).start()


    mark("m11_waitc")
    arrived(cotr, sc.at[0], rc.at[0])
    mark("m12_pack")
    if folds > 1:
        pieces = [cotr[s].astype(F32) for s in range(groups)]
        left = jnp.concatenate(
            [
                jnp.concatenate(
                    [piece[:, f * slots : (f + 1) * slots] for piece in pieces], axis=1
                )
                for f in range(folds)
            ],
            axis=0,
        ).astype(BF16)
        cot_t[...] = dot(left, spread[...]).astype(BF16)
    else:
        cot_t[...] = jnp.zeros(cot_t.shape, BF16)

        def place(s, carry):
            spread[...] = jnp.where(
                slot_row == slot_rows[pl.ds(s, 1), :], 1.0, 0.0
            ).astype(BF16)
            cot_t[...] = cot_t[...] + dot(cotr[s], spread[...]).astype(BF16)
            return carry

        lax.fori_loop(0, groups, place, 0)

    mark("m13_waita")
    for k in direct[::-1]:
        remote(attall.at[me], attall.at[me], sa.at[0], ra.at[k // 2], k).wait_recv()
        piece = attall.at[partner(me, k)]
        remote(piece, piece, sa.at[0], ra.at[0], 1).start()
    exchange(sendg, recvg, sg.at[0], rg.at[0])
    half = attall.at[pl.ds(0, groups // 2)]
    remote(half, half, sa.at[0], ra.at[0], 1).wait_recv()
    mark("m14_wg")
    att_rows = attall[...].reshape(every, hf)
    own[...] = dot(cot_t[...], att_rows).reshape(own.shape)

    def backward():
        mark("m09_waitg")
        arrived(recvg, sg.at[0], rg.at[0])
        mark("m10_bwd")
        xg = dot(pack_t[...], flat(recvg[...]), TN).astype(BF16)
        for h in range(HEADS):
            gbig[h * pack : (h + 1) * pack, :] = xg * marks[h]
        prob_grad = dot(values, gbig[...], NT)
        delta = jnp.sum(probs * prob_grad, axis=0, keepdims=True)
        score_grad = (probs * (prob_grad - delta) * scale).astype(BF16)
        grads[:, :hf] = per_head(dot(score_grad, keys, TN))
        grads[:, hf : 2 * hf] = dot(score_grad, qbig[...]).astype(BF16)
        grads[:, 2 * hf :] = dot(probs_b, gbig[...]).astype(BF16)

        backs[...] = dot(pack_t[...], grads[...]).reshape(groups, SLOT, feats3).astype(BF16)
        exchange(backs, backr, sb.at[0], rb.at[0])


    def project():
        mark("m16_emb")
        emb[...] = dot(dot(home, att_rows).astype(BF16), w[...], NT).astype(BF16)

    def source_rows():
        mark("m17_waitb")
        arrived(backr, sb.at[0], rb.at[0])
        mark("m18_back")
        grad[...] = dot(sel[...], flat(backr[...]), TN).astype(BF16)
        mark("m19_z")

    def along_line():
        mark("m15_zchain")
        @pl.when(rep == 0)
        def _():
            zbuf[0] = jnp.zeros(zbuf.shape[1:], BF16)

        @pl.when(rep == reps - 1)
        def _():
            zbuf[1] = jnp.zeros(zbuf.shape[1:], BF16)

        def hop(way, c):
            return pltpu.make_async_remote_copy(
                src_ref=zsend.at[way, c], dst_ref=zbuf.at[way, c],
                send_sem=sz.at[way], recv_sem=rz.at[way, c],
                device_id={"dp": rep + 1 - 2 * way}, device_id_type=MESH,
            )

        def step(way, c):
            spot = rep + way * (reps - 1 - 2 * rep)

            @pl.when(spot > 0)
            def _():
                hop(way, c).wait_recv()

            @pl.when(spot < reps - 1)
            def _():
                zsend[way, c] = (own[c] + zbuf[way, c].astype(F32)).astype(BF16)
                hop(way, c).start()

        near = (rep >= (reps + 1) // 2).astype(jnp.int32)
        edge = (rep == 0) | (rep == reps - 1)

        @pl.when(edge)
        def _():
            for c in range(chunks):
                step(near, c)

        backward()
        project()

        @pl.when(edge)
        def _():
            source_rows()
            for c in range(chunks):
                step(1 - near, c)

        @pl.when(jnp.logical_not(edge))
        def _():
            mark("m19_zmid")
            lag = chunks // 2
            for t in range(chunks + lag):
                if t < chunks:
                    step(near, t)
                if t >= lag:
                    step(1 - near, t - lag)
            source_rows()

        mark("m20_final")
        own[...] = own[...] + zbuf[0].astype(F32) + zbuf[1].astype(F32)

        for way in range(2):
            spot = rep + way * (reps - 1 - 2 * rep)

            @pl.when(spot < reps - 1)
            def _():
                pltpu.make_async_remote_copy(
                    src_ref=zsend.at[way], dst_ref=zbuf.at[way],
                    send_sem=sz.at[way], recv_sem=rz.at[way, 0],
                    device_id={"dp": rep + 1 - 2 * way}, device_id_type=MESH,
                ).wait_send()


    def by_blocks():
        size = chunks // reps
        cuts = [0, CUT, size] if size > CUT else [0, size]
        spans = list(zip(cuts[:-1], cuts[1:]))
        rounds = len(spans)

        def across(src, dst, i, to):
            return pltpu.make_async_remote_copy(
                src_ref=src, dst_ref=dst, send_sem=sz.at[i], recv_sem=rz.at[i, 0],
                device_id={"dp": to}, device_id_type=MESH,
            )

        mark("m15_scatter")
        pl.semaphore_wait(known.at[reps - 3], peers)
        zsend[0] = own[...].astype(BF16)
        for i, (low, high) in enumerate(spans):
            for to in [reps - 1] + list(range(reps - 1)):

                @pl.when(rep != to)
                def _():
                    across(
                        zsend.at[0, pl.ds(to * size + low, high - low)],
                        zbuf.at[0, pl.ds(low * reps + rep * (high - low), high - low)],
                        i, to,
                    ).start()

        project()
        for i, (low, high) in enumerate(spans):
            wide = high - low
            mark(f"m17_waits{i}")
            most = zbuf.at[0, pl.ds(0, wide * (reps - 1))]
            across(most, most, i, rep).wait_recv()
            mark(f"m18_sum{i}")
            mine = pl.ds(rep * size + low, wide)
            zbuf[0, pl.ds(low * reps + rep * wide, wide)] = jnp.zeros(
                (wide,) + zbuf.shape[2:], BF16
            )
            total = own[mine]
            for r in range(reps):
                first = low * reps + r * wide
                total = total + zbuf[0, first : first + wide].astype(F32)
            zbuf[1, mine] = total.astype(BF16)
            for to in [0, reps - 1] + list(range(1, reps - 1)):

                @pl.when(rep != to)
                def _():
                    across(zbuf.at[1, mine], zbuf.at[1, mine], rounds + i, to).start()
            if i == 0:
                backward()

        source_rows()
        for i, (low, high) in enumerate(spans):
            most = zbuf.at[0, pl.ds(0, (high - low) * (reps - 1))]
            across(most, most, rounds + i, rep).wait_recv()
        mark("m20_final")
        own[...] = zbuf[1].astype(F32)
        for i in range(2 * rounds):
            low, high = spans[i % rounds]
            most = zbuf.at[0, pl.ds(0, (high - low) * (reps - 1))]
            across(most, most, i, rep).wait_send()

    if blocked:
        by_blocks()
    else:
        along_line()

    mark("m21_drain")
    departed(sendg, sg.at[0], rg.at[0])
    departed(cots, sc.at[0], rc.at[0])
    departed(backs, sb.at[0], rb.at[0])
    departed(attall, sa.at[0], ra.at[0])
    mark(None)


def write_out(emb, grad, own, emb_hbm, grad_hbm, wg_hbm, sems):
    pairs = ((emb, emb_hbm), (grad, grad_hbm), (own, wg_hbm))
    copies = [
        pltpu.make_async_copy(src, dst, sems.at[i]) for i, (src, dst) in enumerate(pairs)
    ]
    for copy in copies:
        copy.start()
    for copy in copies:
        copy.wait()


def local(groups, reps, qkv, embed_grad, out_weight, image_len, image_order, image_cut):
    rows, feats3 = qkv.shape
    width, hf = out_weight.shape
    slots = groups * SLOT
    pack = slots // 2
    share = width // groups
    part = 8 if share % (8 * reps) == 0 or share % 16 else 16
    chunks = share // part
    folds = 2 if slots < 128 and share % 32 == 0 else 1
    any_space = pl.BlockSpec(memory_space=pl.ANY)
    vmem = pl.BlockSpec(memory_space=pltpu.VMEM)
    dma = pltpu.SemaphoreType.DMA
    emb, grad, wg = pl.pallas_call(
        functools.partial(kernel, groups, reps),
        out_shape=(
            pltpu.VMEM((rows, width), BF16),
            pltpu.VMEM((rows, feats3), BF16),
            pltpu.VMEM((chunks, part, hf), F32),
        ),
        in_specs=[any_space] * 6,
        out_specs=(vmem, vmem, vmem),
        scratch_shapes=[
            pltpu.VMEM((groups, groups), jnp.int32),
            pltpu.VMEM((1, groups), jnp.int32),
            pltpu.VMEM((1, 1), jnp.int32),
            pltpu.VMEM((rows, feats3), BF16),
            pltpu.VMEM((rows, width), BF16),
            pltpu.VMEM((width, hf), BF16),
            pltpu.VMEM((slots, rows), BF16),
            pltpu.VMEM((slots, pack), BF16),
            pltpu.VMEM((groups, SLOT, feats3), BF16),
            pltpu.VMEM((groups, SLOT, feats3), BF16),
            pltpu.VMEM((groups, SLOT, hf), BF16),
            pltpu.VMEM((groups, SLOT, hf), BF16),
            pltpu.VMEM((groups, share // folds, slots * folds), BF16),
            pltpu.VMEM((groups, share // folds, slots * folds), BF16),
            pltpu.VMEM((HEADS * pack, hf), BF16),
            pltpu.VMEM((HEADS * pack, hf), BF16),
            pltpu.VMEM((groups, pack, hf), BF16),
            pltpu.VMEM((pack, feats3), BF16),
            pltpu.VMEM((groups, SLOT, feats3), BF16),
            pltpu.VMEM((groups, SLOT, feats3), BF16),
            pltpu.VMEM((share, groups * pack), BF16),
            pltpu.VMEM((groups * slots if folds > 1 else slots, groups * pack), BF16),
            pltpu.VMEM((groups, groups * pack), F32),
            pltpu.VMEM((2, chunks, part, hf), BF16),
            pltpu.VMEM((2, chunks, part, hf), BF16),
            dma((6,)),
        ]
        + [dma((1,)) for _ in range(6)]
        + [dma((1,)), dma((groups // 2,)), dma((1,)), dma((1,))]
        + ([dma((4,)), dma((4, 1))] if chunks % reps == 0 else [dma((2,)), dma((2, chunks))])
        + [pltpu.SemaphoreType.REGULAR((max(reps - 2, 1),))],
        compiler_params=pltpu.CompilerParams(
            collective_id=0, has_side_effects=True, vmem_limit_bytes=60 * 1024 * 1024
        ),
    )(
        image_len.reshape(groups, groups), image_order.reshape(1, groups), image_cut,
        qkv, embed_grad, out_weight,
    )
    emb, grad, wg = pl.pallas_call(
        write_out,
        out_shape=(
            jax.ShapeDtypeStruct((rows, width), BF16),
            jax.ShapeDtypeStruct((rows, feats3), BF16),
            jax.ShapeDtypeStruct((chunks, part, hf), F32),
        ),
        in_specs=[vmem, vmem, vmem],
        out_specs=(any_space, any_space, any_space),
        scratch_shapes=[dma((3,))],
    )(*(pltpu.with_memory_space_constraint(x, pltpu.VMEM) for x in (emb, grad, wg)))
    return emb, grad, wg.reshape(share, hf)


def solution(mesh):
    return jax.shard_map(
        functools.partial(local, mesh.shape["group"], mesh.shape["dp"]),
        mesh=mesh,
        in_specs=(
            P(("dp", "group"), None),
            P(("dp", "group"), None),
            P(),
            P("dp", None, None),
            P("dp", "group", None),
            P("dp", "group"),
        ),
        out_specs=(P(("dp", "group"), None), P(("dp", "group"), None), P("group", None)),
        check_vma=False,
    )
```
